32 devices in a mesh: parts: 2 (over x), seq: 16 (over z, y, core).
Axes of the slice: x: 2, y: 2, z: 4, core: 2. Of those that a mesh axis runs over, the one named last changes fastest.
Arguments:
- queries: bfloat16 [4096, 1024], P(('parts', 'seq')), parts along dimension 0, may hold values from -6 to 6
- keys: bfloat16 [4096, 1024], P(('parts', 'seq')), parts along dimension 0, may hold values from -6 to 6
- values: bfloat16 [4096, 1024], P(('parts', 'seq')), parts along dimension 0, may hold values from -6 to 6
- log_forget: float32 [8, 4096], P(None, ('parts', 'seq')), parts along dimension 1, may hold values from -5 to 0
- input_gate: float32 [8, 4096], P(None, ('parts', 'seq')), parts along dimension 1, may hold values from 0.1 to 1
- ridge: float32 [8], replicated, may hold values from 0.25 to 4
- gain: float32 [1024], replicated, may hold values from 0.25 to 1.75
- out_weight: bfloat16 [1024, 2048], P('seq'), may hold values from -0.1875 to 0.1875
Outputs:
- mixed: bfloat16 [4096, 2048], P(('parts', 'seq')), parts along dimension 0
The draws below stay inside these ranges and needn't reach their ends.
There are 2 independent parts, one for each index of `parts`. The reference program is written for one: setup_inputs(seed, part) draws one part's arguments, and reference() takes and returns one part's arrays. A program takes and returns all parts, laid end to end along the dimension named above; an argument that names none is the same for every part. Nothing has to cross between parts.
All inputs are finite; a program needn't handle non-finite values. Where the reference program divides by a largest or mean magnitude, that divisor is 1e-20 or more.
Results may differ from the reference program's by a relative error of at most 0.007.
Values may be sent and summed in bfloat16 or wider, within the bound.
No kernel may reach another device: no remote copies, remote signals or barrier semaphores. Data moves between devices by JAX's collectives and lax.ppermute only.
A program may use at most 192 MiB of HBM per device.

```python
import math
import jax
import jax.numpy as jnp
from jax import lax

D = 2048
HEADS = 8
DH = 128
C = 128
NEWTON = 6
CORR = 4
TOK_DEV = 128
SEQ = 2048
HD = 1024


def draw_log_forget(key, part):
    streams = jax.random.split(jax.random.fold_in(key, 71), 6)
    order = jax.random.permutation(streams[0], HEADS)
    half = HEADS // 2
    sections = SEQ // TOK_DEV
    slow_rate = jnp.exp(jax.random.uniform(streams[1], (HEADS,), jnp.float32, math.log(0.1), math.log(0.6))) / SEQ
    spread_count = max(HEADS - half - 1, 1)
    rank = jnp.maximum(order - half, 0).astype(jnp.float32) / spread_count
    quick_rate = jnp.exp(math.log(14.0) + rank * (math.log(0.5) - math.log(14.0))) / TOK_DEV
    is_slow = order < half
    rate = jnp.where(is_slow, slow_rate, quick_rate)
    section_scale = jnp.exp(jax.random.uniform(streams[2], (HEADS, sections, 1), jnp.float32, math.log(0.5), math.log(2.0)))
    token_scale = jnp.exp(jax.random.uniform(streams[3], (HEADS, sections, TOK_DEV), jnp.float32, math.log(0.5), math.log(2.0)))
    starting_offset = -(rate[:, None, None] * section_scale * token_scale).reshape(HEADS, SEQ)
    sample_locations = jax.random.randint(streams[4], (HEADS, 2), 0, SEQ)
    loss_values = jnp.log(jax.random.uniform(streams[5], (HEADS, 2), jnp.float32, 0.5, 0.8))
    token_positions = jnp.arange(SEQ)[None, :]
    token_group = jnp.where(token_positions == sample_locations[:, 0:1], loss_values[:, 0:1], 0.0) + jnp.where(token_positions == sample_locations[:, 1:2], loss_values[:, 1:2], 0.0)
    return starting_offset + token_group


def levels(key, shape, cuts, low, top_value):
    def one(dim, shards_of):
        heights = jax.random.uniform(jax.random.fold_in(jax.random.fold_in(key, 6), dim), (shards_of,), jnp.float32, low / len(cuts), top_value / len(cuts))
        return jnp.repeat(jnp.exp(heights), shape[dim] // shards_of).reshape((-1,) + (1,) * (len(shape) - dim - 1))

    level = one(*cuts[0])
    for cut in cuts[1:]:
        level = level * one(*cut)
    return level


def scatter_about(stream_key, dims, scale, limit, shards=(), kind=jnp.bfloat16):
    drawn = jax.random.normal(stream_key, dims, jnp.float32) * scale
    if len(shards) > 0:
        drawn = levels(stream_key, dims, shards, -0.22, 0.18) * drawn
    return jnp.clip(drawn, min=-limit, max=limit).astype(kind)


def setup_inputs(seed: int = 0, part: int = 0) -> dict:
    streams_of = jax.random.split(jax.random.key(seed), 9)
    part_keys = jax.random.split(jax.random.fold_in(streams_of[8], part), 9)
    queries = scatter_about(part_keys[0], (SEQ, HD), 1.0, 6.0, ((0, 16),))
    keys = scatter_about(part_keys[1], (SEQ, HD), 1.0, 6.0, ((0, 16),))
    values = scatter_about(part_keys[2], (SEQ, HD), 1.0, 6.0, ((0, 16),))
    log_forget = draw_log_forget(jax.random.fold_in(jax.random.fold_in(streams_of[8], part), 71), part)
    input_gate = jnp.clip(0.1 + 0.9 * jax.random.uniform(part_keys[4], (HEADS, SEQ), jnp.float32) ** levels(part_keys[4], (HEADS, SEQ), ((1, 16),), -0.2, 0.2), 0.1, 1.0)
    ridge = jnp.clip(jnp.exp(jax.random.uniform(streams_of[5], (HEADS,), jnp.float32, math.log(0.25), math.log(4.0))), 0.25, 4.0)
    gain = jnp.clip(1.0 + 0.15 * jax.random.normal(streams_of[6], (HD,), jnp.float32), 0.25, 1.75)
    out_weight = scatter_about(streams_of[7], (HD, D), HD ** -0.5, 0.1875, ((0, 16),))
    return dict(queries=queries, keys=keys, values=values, log_forget=log_forget, input_gate=input_gate, ridge=ridge, gain=gain, out_weight=out_weight)


highest = lax.Precision.HIGHEST

def product(left, right):
    return jnp.matmul(left, right, precision=highest)

def unit_rows(field):
    return field * lax.rsqrt(lax.optimization_barrier(jnp.sum(field * field, axis=-1, keepdims=True)) + 1e-06)

def newton_inverse(system):
    bound = lax.optimization_barrier(jnp.max(lax.optimization_barrier(jnp.sum(jnp.abs(system), axis=-1)), axis=-1))
    identity = jnp.eye(system.shape[-1], dtype=system.dtype)
    approx = identity / bound[..., None, None]
    for iteration in range(NEWTON):
        approx = product(approx, 2.0 * identity - product(system, approx))
    return approx

def solve_block(query_rows, key_rows, beta_keys, start_gram, pre_gram, decay_row, mixing, ridge_col):
    identity = jnp.eye(query_rows.shape[-1], dtype=query_rows.dtype)
    system = start_gram + pre_gram + ridge_col * identity
    inverse = newton_inverse(system)
    solved = product(query_rows, inverse)
    key_t = jnp.swapaxes(key_rows, -1, -2)
    for iteration in range(CORR - 1):
        attention_scores = mixing * product(solved, key_t)
        applied = decay_row * product(solved, start_gram) + product(attention_scores, beta_keys) + ridge_col * solved
        solved = solved + product(query_rows - applied, inverse)
    attention_scores = mixing * product(solved, key_t)
    return (solved, attention_scores)

def reference(queries, keys, values, log_forget, input_gate, ridge, gain, out_weight):
    total = queries.shape[0]
    count = total // C

    def blocks(field):
        return field.astype(jnp.float32).reshape(count, C, HEADS, DH).transpose(0, 2, 1, 3)

    def gate_blocks(field):
        return field.reshape(HEADS, count, C).transpose(1, 0, 2)
    query_all = unit_rows(blocks(queries))
    key_all = unit_rows(blocks(keys))
    value_all = blocks(values)
    forget_all = gate_blocks(log_forget)
    beta_all = gate_blocks(input_gate)
    lower_mask = jnp.tril(jnp.ones((C, C), query_all.dtype))
    ridge_col = ridge[:, None, None]

    def advance(carry, items):
        gram_sum, state_sum = carry
        query_rows, key_rows, value_rows, forget_rows, gate_rows = items
        running = jnp.cumsum(forget_rows, axis=-1)
        last = running[:, -1:]
        decay_row = jnp.exp(running)[..., None]
        mixing = lower_mask * jnp.exp(jnp.minimum(running[:, :, None] - running[:, None, :], 0.0))
        tail = (jnp.exp(last - running) * gate_rows)[..., None]
        beta_keys = gate_rows[..., None] * key_rows
        beta_values = gate_rows[..., None] * value_rows
        key_t = jnp.swapaxes(key_rows, -1, -2)
        block_gram = product(key_t, tail * key_rows)
        state_per_block = product(key_t, tail * value_rows)
        pre_gram = product(key_t, beta_keys)
        solved, attention_scores = solve_block(query_rows, key_rows, beta_keys, gram_sum, pre_gram, decay_row, mixing, ridge_col)
        output = decay_row * product(solved, state_sum) + product(attention_scores, beta_values)
        shrink = jnp.exp(last)[..., None]
        return ((shrink * gram_sum + block_gram, shrink * state_sum + state_per_block), output)
    start = (jnp.zeros((HEADS, DH, DH), query_all.dtype), jnp.zeros((HEADS, DH, DH), query_all.dtype))
    carry, outputs = lax.scan(advance, start, (query_all, key_all, value_all, forget_all, beta_all))
    normed = outputs * lax.rsqrt(lax.optimization_barrier(jnp.mean(outputs * outputs, axis=-1, keepdims=True)) + 1e-06)
    normed = normed.transpose(0, 2, 1, 3).reshape(total, HEADS * DH) * gain
    normed = normed.astype(jnp.bfloat16)
    return jnp.dot(normed, out_weight, preferred_element_type=jnp.float32).astype(jnp.bfloat16)
```

```python
import functools
import jax
import jax.numpy as jnp
from jax import lax
from jax.experimental import pallas as pl
from jax.experimental.pallas import tpu as pltpu
from jax.sharding import PartitionSpec as P

NEWTON = 6
CORR = 4
F32 = jnp.float32
BF16 = jnp.bfloat16
EXACT = lax.Precision.HIGHEST
VMEM_BYTES = 56 * 1024 * 1024


def rows_of(shape):
    return lax.broadcasted_iota(jnp.int32, shape, 0)


def lanes_of(shape):
    return lax.broadcasted_iota(jnp.int32, shape, 1)


def split(x):
    high = x.astype(BF16)
    return high, (x - high.astype(F32)).astype(BF16)


def dot(a, b):
    return jnp.dot(a, b, preferred_element_type=F32)


def dot_t(a, b):
    return lax.dot_general(a, b, (((0,), (0,)), ((), ())), preferred_element_type=F32)


def wide(pair):
    high, low = pair
    return jnp.concatenate([high, low, high], axis=1)


def tall(pair):
    high, low = pair
    return jnp.concatenate([high, high, low], axis=0)


def unit_rows(x):
    return x * lax.rsqrt(jnp.sum(x * x, axis=-1, keepdims=True) + 1e-6)


def pick(first, own, other):
    return jnp.where(first, own, other)


def gates(own_ref, other_ref, core, half):
    own, other = own_ref[...], other_ref[...]
    return jnp.concatenate(
        [
            jnp.where(core == 0, own[:half], own[half:]),
            jnp.where(core == 0, other[:half], other[half:]),
        ],
        axis=0,
    )


def running_sum(a):
    width = a.shape[-1]
    tri = (rows_of((width, width)) <= lanes_of((width, width))).astype(F32)
    return jnp.dot(a, tri, precision=EXACT, preferred_element_type=F32)


def pack(sym):
    width = sym.shape[0]
    half = width // 2
    top, low = sym[:half], pltpu.roll(sym[half:], half, 1)
    shape = (half, width)
    r, c = rows_of(shape), lanes_of(shape)
    body = jnp.where(r > c, low, top)
    diag = jnp.sum(jnp.where(r == c, low, 0.0), axis=0, keepdims=True)
    return body, diag


def unpack(body, diag):
    half, width = body.shape
    r, c = rows_of(body.shape), lanes_of(body.shape)
    top = jnp.where(c > r, body, 0.0) + jnp.where(c == r, 0.5 * body, 0.0)
    low = jnp.where(c < r, body, 0.0) + jnp.where(c == r, 0.5 * diag, 0.0)
    full = jnp.concatenate([top, pltpu.roll(low, half, 1)], axis=0)
    return full + full.T


def tail_rows(diag, level):
    r = rows_of((8, diag.shape[-1]))
    return jnp.where(r == 0, diag, jnp.where(r == 1, level, 0.0))


def tail_sent(diag, level):
    one = level.astype(BF16).astype(F32)
    two = (level - one).astype(BF16).astype(F32)
    three = level - one - two
    r = rows_of((16, diag.shape[-1]))
    out = jnp.where(r == 0, diag, jnp.where(r == 1, one, jnp.where(r == 2, two, jnp.where(r == 3, three, 0.0))))
    return out.astype(BF16)


def sums_kernel(meta, ko, kr, vo, vr, fo, fr, go, gr, pg, tg, pw, tw, gf, uf):
    half = gf.shape[0]
    width = gf.shape[1]
    body = width // 2
    core = meta[0]
    forget = gates(fo, fr, core, half)
    beta = gates(go, gr, core, half)
    level = running_sum(forget)
    last = level[:, width - 1 :]
    tails = (jnp.exp(last - level) * beta).T
    decay = jnp.exp(last)
    first = core == 0
    for h in range(half):
        cols = slice(h * width, (h + 1) * width)
        grams, states = [], []
        for side, (kref, vref) in enumerate(((ko, vo), (kr, vr))):
            p = h + side * half
            k = unit_rows(kref[:, cols].astype(F32))
            tk = split(k * tails[:, p : p + 1])
            kk = split(k)
            v = vref[:, cols]
            grams.append(
                dot_t(jnp.concatenate([tk[0], tk[1], tk[0]], axis=0), jnp.concatenate([kk[0], kk[0], kk[1]], axis=0))
            )
            states.append(dot_t(jnp.concatenate([tk[0], tk[1]], axis=0), jnp.concatenate([v, v], axis=0)))
        early = pick(first, grams[0], grams[1])
        late = pick(first, grams[1], grams[0])
        early_state = pick(first, states[0], states[1])
        late_state = pick(first, states[1], states[0])
        shrink = pick(first, decay[half + h : half + h + 1], decay[h : h + 1])
        gf[h] = early
        uf[h] = early_state
        packed, diag = pack(shrink * early + late)
        total = jnp.broadcast_to(last[h : h + 1] + last[half + h : half + h + 1], (1, width))
        tg[h, :body] = packed
        tg[h, body:] = tail_rows(diag, total)
        pg[h, :body] = packed.astype(BF16)
        pg[h, body:] = tail_sent(diag, total)
        state = shrink * early_state + late_state
        tw[h] = state
        pw[h] = state.astype(BF16)


def join_kernel(which, has_prefix, meta, t, got, *rest):
    if has_prefix:
        before, t_new, sent, before_new, coef = rest
    else:
        t_new, sent, before_new, coef = rest
    bit = meta[which] == 1
    half, rows, width = t.shape
    body = rows - 8
    for h in range(half):
        tail = t[h, body:]
        mine = tail[1:2]
        ends = got[h, body:].astype(F32)
        theirs = ends[1:2] + ends[2:3] + ends[3:4]
        a = jnp.where(bit, 1.0, jnp.exp(theirs))
        b = jnp.where(bit, jnp.exp(mine), 1.0)
        arrived = got[h, :body].astype(F32)
        packed = a * t[h, :body] + b * arrived
        diag = a * tail[:1] + b * ends[:1]
        t_new[h, :body] = packed
        t_new[h, body:] = tail_rows(diag, mine + theirs)
        sent[h, :body] = packed.astype(BF16)
        sent[h, body:] = tail_sent(diag, mine + theirs)
        if has_prefix:
            old = before[h, body:]
            e = jnp.where(bit, jnp.exp(old[1:2]), 0.0)
            before_new[h, :body] = before[h, :body] + e * arrived
            before_new[h, body:] = tail_rows(old[:1] + e * ends[:1], old[1:2] + jnp.where(bit, theirs, 0.0))
        else:
            e = jnp.where(bit, jnp.ones_like(mine), 0.0)
            before_new[h, :body] = e * arrived
            before_new[h, body:] = tail_rows(e * ends[:1], jnp.where(bit, theirs, 0.0))
        r = rows_of((8, width))
        coef[h] = jnp.where(r == 0, a, jnp.where(r == 1, b, jnp.where(r == 2, e, 0.0)))


def join_state_kernel(has_prefix, coef, t, got, *rest):
    if has_prefix:
        before, t_new, sent, before_new = rest
    else:
        t_new, sent, before_new = rest
    for h in range(t.shape[0]):
        c = coef[h]
        arrived = got[h].astype(F32)
        new = c[0:1] * t[h] + c[1:2] * arrived
        t_new[h] = new
        sent[h] = new.astype(BF16)
        add = c[2:3] * arrived
        before_new[h] = before[h] + add if has_prefix else add


def solve_kernel(
    which, meta, ridge, ko, kr, qo, qr, vo, vr, fo, fr, go, gr, gf, before, got, xs, part,
    q_s, s_s, m_s, k_s, a_s, p_s, e_s, x_s,
):
    half = gf.shape[0]
    width = gf.shape[1]
    body = width // 2
    pairs = 2 * half
    core = meta[0]
    first = core == 0
    bit = meta[which] == 1
    forget = gates(fo, fr, core, half)
    beta = gates(go, gr, core, half)
    level = running_sum(forget)
    decay = jnp.exp(level[:, width - 1 :])
    level_t = level.T
    beta_t = beta.T
    square = (width, width)
    lower = rows_of(square) >= lanes_of(square)
    eye = (rows_of(square) == lanes_of(square)).astype(F32)
    sides = ((ko, qo, first), (kr, qr, jnp.logical_not(first)))
    for h in range(half):
        cols = slice(h * width, (h + 1) * width)
        tail = before[h, body:]
        ends = got[h, body:].astype(F32)
        e = jnp.where(bit, jnp.exp(tail[1:2]), 0.0)
        start = unpack(before[h, :body] + e * got[h, :body].astype(F32), tail[:1] + e * ends[:1])
        for side, (kref, qref, is_early) in enumerate(sides):
            p = h + side * half
            other = h + (1 - side) * half
            k = unit_rows(kref[:, cols].astype(F32))
            gram = jnp.where(is_early, start, decay[other : other + 1] * start + gf[h])
            sh, sl = split(gram)
            kh, kl = split(k)
            kth, ktl = split(k.T)
            s_s[p, 0, :, :width] = sh
            s_s[p, 1, :, :width] = sl
            s_s[p, 0, :, width:] = kth
            s_s[p, 1, :, width:] = ktl
            k_s[p, 0] = kh
            k_s[p, 1] = kl
            bk = split(k * beta_t[:, p : p + 1])
            cross = dot_t(jnp.concatenate([bk[0], bk[1], bk[0]], axis=0), jnp.concatenate([kh, kh, kl], axis=0))
            system = gram + cross + ridge[core * half + h] * eye
            bound = jnp.max(jnp.sum(jnp.abs(system), axis=0, keepdims=True), axis=1, keepdims=True)
            ah, al = split(system)
            a_s[p, 0] = ah
            a_s[p, 1] = al
            p_s[p] = eye / bound
            column = level_t[:, p : p + 1]
            m_s[p] = jnp.where(lower, jnp.exp(jnp.minimum(column - level[p : p + 1], 0.0)) * beta[p : p + 1], 0.0)
            e_s[p] = jnp.broadcast_to(jnp.exp(column), square)
            q_s[p] = unit_rows(qref[:, cols].astype(F32))

    def refine(_, carry):
        left = [eye - dot(a_s[p, 0], p_s[p].astype(BF16)) for p in range(pairs)]
        for p in range(pairs):
            now = p_s[p]
            p_s[p] = now + dot(now.astype(BF16), left[p].astype(BF16))
        return carry

    lax.fori_loop(0, NEWTON - 1, refine, 0)
    for base in range(0, pairs, half):
        group = range(base, base + half)
        left = []
        for p in group:
            left.append(eye - dot(wide((a_s[p, 0], a_s[p, 1])), tall(split(p_s[p]))))
        for p, rest in zip(group, left):
            now = p_s[p]
            p_s[p] = now + dot(wide(split(now)), tall(split(rest)))

    for p in range(pairs):
        x_s[p] = dot(q_s[p].astype(BF16), p_s[p].astype(BF16))

    def correct(_, carry):
        both = [dot(x_s[p].astype(BF16), s_s[p, 0]) for p in range(pairs)]
        applied = []
        for p in range(pairs):
            scores = m_s[p] * both[p][:, width:]
            h = p % half
            applied.append(
                e_s[p] * both[p][:, :width]
                + dot(scores.astype(BF16), k_s[p, 0])
                + ridge[core * half + h] * x_s[p]
            )
        for p in range(pairs):
            x_s[p] = x_s[p] + dot((q_s[p] - applied[p]).astype(BF16), p_s[p].astype(BF16))
        return carry

    lax.fori_loop(0, CORR - 2, correct, 0)

    for base, vref in ((0, vo), (half, vr)):
        group = range(base, base + half)
        both = [dot(wide(split(x_s[p])), tall((s_s[p, 0], s_s[p, 1]))) for p in group]
        applied = []
        for p, found in zip(group, both):
            scores = m_s[p] * found[:, width:]
            applied.append(
                e_s[p] * found[:, :width]
                + dot(wide(split(scores)), tall((k_s[p, 0], k_s[p, 1])))
                + ridge[core * half + p - base] * x_s[p]
            )
        solved = []
        for p, found in zip(group, applied):
            x = x_s[p] + dot((q_s[p] - found).astype(BF16), p_s[p].astype(BF16))
            solved.append(split(x))
            xs[p, 0], xs[p, 1] = solved[-1]
        scores = []
        for p, x in zip(group, solved):
            kt = (s_s[p, 0, :, width:], s_s[p, 1, :, width:])
            scores.append(m_s[p] * dot(wide(x), tall(kt)))
        for p, found in zip(group, scores):
            h = p - base
            v = vref[:, h * width : (h + 1) * width]
            sh, sl = split(found)
            part[p] = dot(jnp.concatenate([sh, sl], axis=1), jnp.concatenate([v, v], axis=0))


def read_kernel(which, meta, xs, part, fo, fr, uf, tail, before, got, gain, y_own, y_other):
    half = uf.shape[0]
    width = uf.shape[1]
    core = meta[0]
    first = core == 0
    bit = meta[which] == 1
    level = running_sum(gates(fo, fr, core, half))
    decay = jnp.exp(level[:, width - 1 :])
    level_t = level.T
    sides = ((y_own, first), (y_other, jnp.logical_not(first)))
    for h in range(half):
        cols = slice(h * width, (h + 1) * width)
        e = jnp.where(bit, jnp.exp(tail[h, 1:2]), 0.0)
        start = before[h] + e * got[h].astype(F32)
        for side, (out, is_early) in enumerate(sides):
            p = h + side * half
            other = h + (1 - side) * half
            state = jnp.where(is_early, start, decay[other : other + 1] * start + uf[h])
            read = dot(wide((xs[p, 0], xs[p, 1])), tall(split(state)))
            o = jnp.exp(level_t[:, p : p + 1]) * read + part[p]
            o = o * lax.rsqrt(jnp.mean(o * o, axis=-1, keepdims=True) + 1e-6)
            out[:, cols] = (o * gain[:, cols]).astype(BF16)


def project_kernel(slabs, meta, y_own, y_other, *rest):
    pieces = rest[: len(slabs)]
    out, w, y, sem = rest[len(slabs) :]
    core = meta[0]
    place = meta[meta.shape[0] - 1]
    copies = []
    for piece, (offsets, flip) in zip(pieces, slabs):
        rows = piece.shape[1]
        for i, offset in enumerate(offsets):
            chip = jnp.bitwise_xor(place, offset)
            row = (chip * 2 + jnp.bitwise_xor(core, flip)) * rows
            copies.append(
                pltpu.make_async_copy(
                    piece.at[i], w.at[pl.ds(pl.multiple_of(row, rows), rows)], sem.at[len(copies)]
                )
            )
    for copy in copies:
        copy.start()
    wide_half = y_own.shape[1]
    y[:, pl.ds(pl.multiple_of(core * wide_half, wide_half), wide_half)] = y_own[...]
    y[:, pl.ds(pl.multiple_of((1 - core) * wide_half, wide_half), wide_half)] = y_other[...]
    for copy in copies:
        copy.wait()
    out[...] = dot(y[...], w[...]).astype(BF16)


def shape(*dims, dtype=F32):
    return jax.ShapeDtypeStruct(dims, dtype)


def whole(array):
    zeros = (0,) * len(array.shape)
    return pl.BlockSpec(array.shape, lambda i, *_: zeros)


def call(kernel, outs, ins, specs, scalars, scratch=()):
    return pl.pallas_call(
        kernel,
        out_shape=outs,
        grid_spec=pltpu.PrefetchScalarGridSpec(
            num_scalar_prefetch=len(scalars),
            grid=(1,),
            in_specs=specs,
            out_specs=jax.tree.map(whole, outs),
            scratch_shapes=scratch,
        ),
        compiler_params=pltpu.CompilerParams(vmem_limit_bytes=VMEM_BYTES),
    )(*scalars, *ins)


def on_device(sections, queries, keys, values, log_forget, input_gate, ridge, gain, out_weight):
    tokens, features = keys.shape
    heads = log_forget.shape[0]
    width = features // heads
    half = heads // 2
    pairs = 2 * half
    body = width // 2
    chips = sections // 2
    bits = chips.bit_length() - 1
    index = lax.axis_index("seq")
    steps = lax.iota(jnp.int32, bits + 2)
    meta = jnp.where(steps == bits + 1, index >> 1, (index >> steps) & 1)

    def swap(array, distance):
        return lax.ppermute(array, "seq", [(i, i ^ distance) for i in range(sections)])

    keys_o, forget_o, gate_o = swap(keys, 1), swap(log_forget, 1), swap(input_gate, 1)
    values_o, queries_o = swap(values, 1), swap(queries, 1)

    my_heads = pl.BlockSpec((tokens, half * width), lambda i, m, *_: (0, m[0]))
    gate_args = (log_forget, forget_o, input_gate, gate_o)
    gate_specs = [whole(a) for a in gate_args]
    packed = (half, body + 8, width)
    sent = (half, body + 16, width)
    full = (half, width, width)

    pg, tg, pw, tw, gf, uf = call(
        sums_kernel,
        (shape(*sent, dtype=BF16), shape(*packed), shape(*full, dtype=BF16), shape(*full), shape(*full), shape(*full)),
        (keys, keys_o, values, values_o, *gate_args),
        [my_heads] * 4 + gate_specs,
        (meta,),
    )

    before = before_w = None
    for round_ in range(bits):
        got = swap(pg, 2 << round_)
        got_w = swap(pw, 2 << round_)
        if round_ == bits - 1:
            break
        extra = () if before is None else (before,)
        ins = (tg, got, *extra)
        tg, pg, before, coef = call(
            functools.partial(join_kernel, round_ + 1, bool(extra)),
            (shape(*packed), shape(*sent, dtype=BF16), shape(*packed), shape(half, 8, width)),
            ins,
            [whole(a) for a in ins],
            (meta,),
        )
        extra = () if before_w is None else (before_w,)
        ins = (coef, tw, got_w, *extra)
        tw, pw, before_w = pl.pallas_call(
            functools.partial(join_state_kernel, bool(extra)),
            out_shape=(shape(*full), shape(*full, dtype=BF16), shape(*full)),
            compiler_params=pltpu.CompilerParams(vmem_limit_bytes=VMEM_BYTES),
        )(*ins)
    last = bits

    own = out_weight[None]
    groups = [((0,), own)]
    held = ((0,), own)
    for bit in reversed(range(1, bits)):
        offsets = tuple(o ^ (1 << bit) for o in held[0])
        groups.append((offsets, swap(held[1], 2 << bit)))
        fresh = groups[-1]
        if bit > 1:
            held = (held[0] + fresh[0], jnp.concatenate([held[1], fresh[1]], axis=0))
    groups.append((tuple(o ^ 1 for o in held[0]), swap(held[1], 2)))
    if bits > 1:
        groups.append((tuple(o ^ 1 for o in fresh[0]), swap(fresh[1], 2)))
    slabs, pieces = [], []
    for offsets, group in groups:
        slabs += [(offsets, 0), (offsets, 1)]
        pieces += [group, swap(group, 1)]

    ins = (keys, keys_o, queries, queries_o, values, values_o, *gate_args, gf, before, got)
    xs, part = call(
        functools.partial(solve_kernel, last),
        (shape(pairs, 2, tokens, width, dtype=BF16), shape(pairs, tokens, width)),
        ins,
        [my_heads] * 6 + gate_specs + [whole(gf), whole(before), whole(got)],
        (meta, ridge),
        [
            pltpu.VMEM((pairs, tokens, width), F32),
            pltpu.VMEM((pairs, 2, width, 2 * width), BF16),
            pltpu.VMEM((pairs, tokens, tokens), F32),
            pltpu.VMEM((pairs, 2, tokens, width), BF16),
            pltpu.VMEM((pairs, 2, width, width), BF16),
            pltpu.VMEM((pairs, width, width), F32),
            pltpu.VMEM((pairs, tokens, width), F32),
            pltpu.VMEM((pairs, tokens, width), F32),
        ],
    )

    tail = pl.BlockSpec((half, 8, width), lambda i, m: (0, body // 8, 0))
    gain_row = gain.reshape(1, features)
    my_gain = pl.BlockSpec((1, half * width), lambda i, m: (0, m[0]))
    ins = (xs, part, log_forget, forget_o, uf, before, before_w, got_w, gain_row)
    y_own, y_other = call(
        functools.partial(read_kernel, last),
        (shape(tokens, half * width, dtype=BF16),) * 2,
        ins,
        [whole(a) for a in ins[:5]] + [tail, whole(before_w), whole(got_w), my_gain],
        (meta,),
    )
    y_got = swap(y_other, 1)

    columns = out_weight.shape[1]
    anywhere = pl.BlockSpec(memory_space=pl.ANY)
    return call(
        functools.partial(project_kernel, slabs),
        shape(tokens, columns, dtype=BF16),
        (y_own, y_got, *pieces),
        [whole(y_own), whole(y_got)] + [anywhere] * len(pieces),
        (meta,),
        [
            pltpu.VMEM((features, columns), BF16),
            pltpu.VMEM((tokens, features), BF16),
            pltpu.SemaphoreType.DMA((sections,)),
        ],
    )


def solution(mesh):
    rows = P(("parts", "seq"), None)
    gate = P(None, ("parts", "seq"))
    return jax.shard_map(
        functools.partial(on_device, mesh.shape["seq"]),
        mesh=mesh,
        in_specs=(rows, rows, rows, gate, gate, P(), P(), P("seq", None)),
        out_specs=rows,
        check_vma=False,
    )
```

```python
import functools
import jax
import jax.numpy as jnp
from jax import lax
from jax.experimental import pallas as pl
from jax.experimental.pallas import tpu as pltpu
from jax.sharding import PartitionSpec as P

NEWTON = 6
CORR = 4
F32 = jnp.float32
BF16 = jnp.bfloat16
EXACT = lax.Precision.HIGHEST
VMEM = pltpu.VMEM
GRANT = 8 * 1024 * 1024


def rows_of(shape):
    return lax.broadcasted_iota(jnp.int32, shape, 0)


def lanes_of(shape):
    return lax.broadcasted_iota(jnp.int32, shape, 1)


def split(x):
    high = x.astype(BF16)
    return high, (x - high.astype(F32)).astype(BF16)


def dot(a, b):
    return jnp.dot(a, b, preferred_element_type=F32)


def dot_t(a, b):
    return lax.dot_general(a, b, (((0,), (0,)), ((), ())), preferred_element_type=F32)


def wide(pair):
    high, low = pair
    return jnp.concatenate([high, low, high], axis=1)


def tall(pair):
    high, low = pair
    return jnp.concatenate([high, high, low], axis=0)


def unit_rows(x):
    return x * lax.rsqrt(jnp.sum(x * x, axis=-1, keepdims=True) + 1e-6)


def pick(first, own, other):
    return jnp.where(first, own, other)


def columns(ref, core, h, half, width):
    return ref[:, pl.ds(pl.multiple_of((core * half + h) * width, width), width)]


def gates(own_ref, other_ref, core, half):
    own, other = own_ref[...], other_ref[...]
    return jnp.concatenate(
        [
            jnp.where(core == 0, own[:half], own[half:]),
            jnp.where(core == 0, other[:half], other[half:]),
        ],
        axis=0,
    )


def running_sum(a):
    width = a.shape[-1]
    tri = (rows_of((width, width)) <= lanes_of((width, width))).astype(F32)
    return jnp.dot(a, tri, precision=EXACT, preferred_element_type=F32)


def pack(sym):
    width = sym.shape[0]
    half = width // 2
    top, low = sym[:half], pltpu.roll(sym[half:], half, 1)
    shape = (half, width)
    r, c = rows_of(shape), lanes_of(shape)
    body = jnp.where(r > c, low, top)
    diag = jnp.sum(jnp.where(r == c, low, 0.0), axis=0, keepdims=True)
    return body, diag


def unpack(body, diag):
    half, _ = body.shape
    r, c = rows_of(body.shape), lanes_of(body.shape)
    top = jnp.where(c > r, body, 0.0) + jnp.where(c == r, 0.5 * body, 0.0)
    low = jnp.where(c < r, body, 0.0) + jnp.where(c == r, 0.5 * diag, 0.0)
    full = jnp.concatenate([top, pltpu.roll(low, half, 1)], axis=0)
    return full + full.T


def tail_rows(diag, level):
    r = rows_of((8, diag.shape[-1]))
    return jnp.where(r == 0, diag, jnp.where(r == 1, level, 0.0))


def tail_sent(diag, level):
    one = level.astype(BF16).astype(F32)
    two = (level - one).astype(BF16).astype(F32)
    three = level - one - two
    r = rows_of((16, diag.shape[-1]))
    out = jnp.where(r == 0, diag, jnp.where(r == 1, one, jnp.where(r == 2, two, jnp.where(r == 3, three, 0.0))))
    return out.astype(BF16)


def sums_kernel(meta, ko, kr, vo, vr, fo, fr, go, gr, pg, tg, pw, tw, gf, uf, ks):
    half = gf.shape[0]
    width = gf.shape[1]
    body = width // 2
    core = meta[0]
    forget = gates(fo, fr, core, half)
    beta = gates(go, gr, core, half)
    level = running_sum(forget)
    last = level[:, width - 1 :]
    tails = (jnp.exp(last - level) * beta).T
    decay = jnp.exp(last)
    first = core == 0
    for h in range(half):
        grams, states = [], []
        for side, (kref, vref) in enumerate(((ko, vo), (kr, vr))):
            p = h + side * half
            k = unit_rows(columns(kref, core, h, half, width).astype(F32))
            tk = split(k * tails[:, p : p + 1])
            kk = split(k)
            ks[p, 0], ks[p, 1] = kk
            v = columns(vref, core, h, half, width)
            grams.append(
                dot_t(jnp.concatenate([tk[0], tk[1], tk[0]], axis=0), jnp.concatenate([kk[0], kk[0], kk[1]], axis=0))
            )
            states.append(dot_t(jnp.concatenate([tk[0], tk[1]], axis=0), jnp.concatenate([v, v], axis=0)))
        early = pick(first, grams[0], grams[1])
        late = pick(first, grams[1], grams[0])
        early_state = pick(first, states[0], states[1])
        late_state = pick(first, states[1], states[0])
        shrink = pick(first, decay[half + h : half + h + 1], decay[h : h + 1])
        gf[h] = early
        uf[h] = early_state
        packed, diag = pack(shrink * early + late)
        total = jnp.broadcast_to(last[h : h + 1] + last[half + h : half + h + 1], (1, width))
        tg[h, :body] = packed
        tg[h, body:] = tail_rows(diag, total)
        pg[h, :body] = packed.astype(BF16)
        pg[h, body:] = tail_sent(diag, total)
        state = shrink * early_state + late_state
        tw[h] = state
        pw[h] = state.astype(BF16)


def join_kernel(which, has_prefix, meta, t, got, *rest):
    if has_prefix:
        before, t_new, sent, before_new, coef = rest
    else:
        t_new, sent, before_new, coef = rest
    bit = meta[which] == 1
    half, rows, width = t.shape
    body = rows - 8
    for h in range(half):
        tail = t[h, body:]
        mine = tail[1:2]
        ends = got[h, body:].astype(F32)
        theirs = ends[1:2] + ends[2:3] + ends[3:4]
        a = jnp.where(bit, 1.0, jnp.exp(theirs))
        b = jnp.where(bit, jnp.exp(mine), 1.0)
        arrived = got[h, :body].astype(F32)
        packed = a * t[h, :body] + b * arrived
        diag = a * tail[:1] + b * ends[:1]
        t_new[h, :body] = packed
        t_new[h, body:] = tail_rows(diag, mine + theirs)
        sent[h, :body] = packed.astype(BF16)
        sent[h, body:] = tail_sent(diag, mine + theirs)
        if has_prefix:
            old = before[h, body:]
            e = jnp.where(bit, jnp.exp(old[1:2]), 0.0)
            before_new[h, :body] = before[h, :body] + e * arrived
            before_new[h, body:] = tail_rows(old[:1] + e * ends[:1], old[1:2] + jnp.where(bit, theirs, 0.0))
        else:
            e = jnp.where(bit, jnp.ones_like(mine), 0.0)
            before_new[h, :body] = e * arrived
            before_new[h, body:] = tail_rows(e * ends[:1], jnp.where(bit, theirs, 0.0))
        r = rows_of((8, width))
        coef[h] = jnp.where(r == 0, a, jnp.where(r == 1, b, jnp.where(r == 2, e, 0.0)))


def join_state_kernel(has_prefix, coef, t, got, *rest):
    if has_prefix:
        before, t_new, sent, before_new = rest
    else:
        t_new, sent, before_new = rest
    for h in range(t.shape[0]):
        c = coef[h]
        arrived = got[h].astype(F32)
        new = c[0:1] * t[h] + c[1:2] * arrived
        t_new[h] = new
        sent[h] = new.astype(BF16)
        add = c[2:3] * arrived
        before_new[h] = before[h] + add if has_prefix else add


def prepare_kernel(meta, ridge, ks, qo, qr, fo, fr, go, gr, q_s, kt, m_s, e_s, base):
    pairs, _, tokens, width = ks.shape
    half = pairs // 2
    core = meta[0]
    beta = gates(go, gr, core, half)
    level = running_sum(gates(fo, fr, core, half))
    level_t = level.T
    beta_t = beta.T
    square = (tokens, tokens)
    lower = rows_of(square) >= lanes_of(square)
    eye = (rows_of((width, width)) == lanes_of((width, width))).astype(F32)
    for side, qref in enumerate((qo, qr)):
        for h in range(half):
            p = h + side * half
            kh, kl = ks[p, 0], ks[p, 1]
            kt[p, 0], kt[p, 1] = kh.T, kl.T
            k = kh.astype(F32) + kl.astype(F32)
            bk = split(k * beta_t[:, p : p + 1])
            cross = dot_t(jnp.concatenate([bk[0], bk[1], bk[0]], axis=0), jnp.concatenate([kh, kh, kl], axis=0))
            base[p] = cross + ridge[core * half + h] * eye
            column = level_t[:, p : p + 1]
            m_s[p] = jnp.where(lower, jnp.exp(jnp.minimum(column - level[p : p + 1], 0.0)) * beta[p : p + 1], 0.0)
            e_s[p] = jnp.broadcast_to(jnp.exp(column), square)
            q_s[p] = unit_rows(columns(qref, core, h, half, width).astype(F32))


def inverse_kernel(which, meta, base, fo, fr, gf, before, got, s_s, p_s, a_s):
    half, width, _ = gf.shape
    body = width // 2
    pairs = 2 * half
    core = meta[0]
    first = core == 0
    bit = meta[which] == 1
    forget = gates(fo, fr, core, half)
    decay = jnp.exp(jnp.sum(forget, axis=1, keepdims=True))
    eye = (rows_of((width, width)) == lanes_of((width, width))).astype(F32)
    for h in range(half):
        tail = before[h, body:]
        ends = got[h, body:].astype(F32)
        e = jnp.where(bit, jnp.exp(tail[1:2]), 0.0)
        start = unpack(before[h, :body] + e * got[h, :body].astype(F32), tail[:1] + e * ends[:1])
        for side, is_early in enumerate((first, jnp.logical_not(first))):
            p = h + side * half
            other = h + (1 - side) * half
            gram = jnp.where(is_early, start, decay[other : other + 1] * start + gf[h])
            s_s[p, 0], s_s[p, 1] = split(gram)
            system = gram + base[p]
            bound = jnp.max(jnp.sum(jnp.abs(system), axis=0, keepdims=True), axis=1, keepdims=True)
            a_s[p, 0], a_s[p, 1] = split(system)
            p_s[p] = eye / bound

    def refine(_, carry):
        left = [eye - dot(a_s[p, 0], p_s[p].astype(BF16)) for p in range(pairs)]
        for p in range(pairs):
            now = p_s[p]
            p_s[p] = now + dot(now.astype(BF16), left[p].astype(BF16))
        return carry

    lax.fori_loop(0, NEWTON - 1, refine, 0)
    for start in range(0, pairs, half):
        group = range(start, start + half)
        left = []
        for p in group:
            left.append(eye - dot(wide((a_s[p, 0], a_s[p, 1])), tall(split(p_s[p]))))
        for p, rest in zip(group, left):
            now = p_s[p]
            p_s[p] = now + dot(wide(split(now)), tall(split(rest)))


def correct_kernel(meta, ridge, q_s, kt, m_s, e_s, ks, s_s, p_s, vo, vr, xs, part, x_s):
    pairs, _, width = q_s.shape
    half = pairs // 2
    core = meta[0]

    def both_of(p, i):
        return jnp.concatenate([s_s[p, i], kt[p, i]], axis=1)

    for p in range(pairs):
        x_s[p] = dot(q_s[p].astype(BF16), p_s[p].astype(BF16))

    def correct(_, carry):
        both = [dot(x_s[p].astype(BF16), both_of(p, 0)) for p in range(pairs)]
        applied = []
        for p in range(pairs):
            scores = m_s[p] * both[p][:, width:]
            applied.append(
                e_s[p] * both[p][:, :width]
                + dot(scores.astype(BF16), ks[p, 0])
                + ridge[core * half + p % half] * x_s[p]
            )
        for p in range(pairs):
            x_s[p] = x_s[p] + dot((q_s[p] - applied[p]).astype(BF16), p_s[p].astype(BF16))
        return carry

    lax.fori_loop(0, CORR - 2, correct, 0)

    for start, vref in ((0, vo), (half, vr)):
        group = range(start, start + half)
        both = [dot(wide(split(x_s[p])), tall((both_of(p, 0), both_of(p, 1)))) for p in group]
        applied = []
        for p, found in zip(group, both):
            scores = m_s[p] * found[:, width:]
            applied.append(
                e_s[p] * found[:, :width]
                + dot(wide(split(scores)), tall((ks[p, 0], ks[p, 1])))
                + ridge[core * half + p - start] * x_s[p]
            )
        solved = []
        for p, found in zip(group, applied):
            x = x_s[p] + dot((q_s[p] - found).astype(BF16), p_s[p].astype(BF16))
            solved.append(split(x))
            xs[p, 0], xs[p, 1] = solved[-1]
        scores = []
        for p, x in zip(group, solved):
            scores.append(m_s[p] * dot(wide(x), tall((kt[p, 0], kt[p, 1]))))
        for p, found in zip(group, scores):
            v = columns(vref, core, p - start, half, width)
            sh, sl = split(found)
            part[p] = dot(jnp.concatenate([sh, sl], axis=1), jnp.concatenate([v, v], axis=0))


def read_kernel(which, meta, xs, part, e_s, fo, fr, uf, before_g, before, got, gain, y_own, y_other):
    half = uf.shape[0]
    width = uf.shape[1]
    body = width // 2
    core = meta[0]
    first = core == 0
    bit = meta[which] == 1
    decay = jnp.exp(jnp.sum(gates(fo, fr, core, half), axis=1, keepdims=True))
    sides = ((y_own, first), (y_other, jnp.logical_not(first)))
    for h in range(half):
        cols = slice(h * width, (h + 1) * width)
        e = jnp.where(bit, jnp.exp(before_g[h, body + 1 : body + 2]), 0.0)
        start = before[h] + e * got[h].astype(F32)
        scale = columns(gain, core, h, half, width)
        for side, (out, is_early) in enumerate(sides):
            p = h + side * half
            other = h + (1 - side) * half
            state = jnp.where(is_early, start, decay[other : other + 1] * start + uf[h])
            read = dot(wide((xs[p, 0], xs[p, 1])), tall(split(state)))
            o = e_s[p] * read + part[p]
            o = o * lax.rsqrt(jnp.mean(o * o, axis=-1, keepdims=True) + 1e-6)
            out[:, cols] = (o * scale).astype(BF16)


def share_kernel(meta, w, out):
    size = out.shape[2]
    share = meta[meta.shape[0] - 1]
    out[0] = w[:, pl.ds(pl.multiple_of(share * size, size), size)]


def stack_kernel(a, b, out):
    out[: a.shape[0]] = a[...]
    out[a.shape[0] :] = b[...]


def gathered_rows(meta, y_own, y_other, y):
    core = meta[0]
    size = y_own.shape[1]
    y[:, pl.ds(pl.multiple_of(core * size, size), size)] = y_own[...]
    y[:, pl.ds(pl.multiple_of((1 - core) * size, size), size)] = y_other[...]


def project_kernel(table, chips, meta, y_own, y_other, own, other, *rest):
    out, y = rest[-2:]
    core = meta[0]
    place = meta[meta.shape[0] - 2]
    share = meta[meta.shape[0] - 1]
    gathered_rows(meta, y_own, y_other, y)
    width = 2 * own.shape[0]
    shares = own.shape[1] // rest[0].shape[2]
    size = rest[0].shape[2]
    tokens = y.shape[0]
    lefts = []
    for offset in range(chips):
        chip = jnp.bitwise_xor(place, offset)
        rows = y[:, pl.ds(pl.multiple_of(chip * width, width), width)].astype(F32)
        rows = jnp.where(core == 0, rows, pltpu.roll(rows, width // 2, 1))
        lefts.append(rows.astype(BF16))
    for q in range(shares):
        where = pl.ds(pl.multiple_of(jnp.bitwise_xor(share, q) * size, size), size)
        total = jnp.zeros((tokens, size), F32)
        for offset in range(0, chips, 2):
            blocks = []
            for o in (offset, offset + 1):
                for flip in (0, 1):
                    if o == 0:
                        blocks.append((own, other)[flip][:, where])
                    else:
                        piece, i = table[o, flip, q]
                        blocks.append(rest[piece][i])
            left = jnp.concatenate([lefts[offset], lefts[offset + 1]], axis=1)
            total = total + dot(left, jnp.concatenate(blocks, axis=0))
        out[:, where] = total.astype(BF16)


def project_copy_kernel(table, meta, y_own, y_other, own, other, *rest):
    pieces = rest[:-4]
    out, w, y, sem = rest[-4:]
    core = meta[0]
    place = meta[meta.shape[0] - 2]
    share = meta[meta.shape[0] - 1]
    rows = own.shape[0]
    size = pieces[0].shape[2]

    def at(offset, flip):
        row = (jnp.bitwise_xor(place, offset) * 2 + jnp.bitwise_xor(core, flip)) * rows
        return pl.ds(pl.multiple_of(row, rows), rows)

    copies = [
        pltpu.make_async_copy(own, w.at[at(0, 0)], sem.at[0]),
        pltpu.make_async_copy(other, w.at[at(0, 1)], sem.at[1]),
    ]
    for (offset, flip, q), (piece, i) in table.items():
        where = pl.ds(pl.multiple_of(jnp.bitwise_xor(share, q) * size, size), size)
        copies.append(
            pltpu.make_async_copy(pieces[piece].at[i], w.at[at(offset, flip), where], sem.at[len(copies)])
        )
    for copy in copies:
        copy.start()
    gathered_rows(meta, y_own, y_other, y)
    for copy in copies:
        copy.wait()
    out[...] = dot(y[...], w[...]).astype(BF16)


SMEM = pltpu.SMEM


def call(kernel, outs, scalars, ins, scratch=()):
    spec = pl.BlockSpec(memory_space=VMEM)
    near = [pltpu.with_memory_space_constraint(a, VMEM) for a in ins]
    return pl.pallas_call(
        kernel,
        out_shape=outs,
        in_specs=[pl.BlockSpec(memory_space=SMEM)] * len(scalars) + [spec] * len(near),
        out_specs=jax.tree.map(lambda _: spec, outs),
        scratch_shapes=scratch,
        compiler_params=pltpu.CompilerParams(vmem_limit_bytes=GRANT),
    )(*scalars, *near)


def on_device(mesh, queries, keys, values, log_forget, input_gate, ridge, gain, out_weight):
    sections, parts = mesh.shape["seq"], mesh.shape["parts"]
    tokens, features = keys.shape
    heads = log_forget.shape[0]
    width = features // heads
    half = heads // 2
    pairs = 2 * half
    body = width // 2
    chips = sections // 2
    bits = chips.bit_length() - 1
    rows, out_columns = out_weight.shape
    index = lax.axis_index("seq")
    steps = lax.iota(jnp.int32, bits + 3)
    meta = jnp.where(
        steps == bits + 2, lax.axis_index("parts"), jnp.where(steps == bits + 1, index >> 1, (index >> steps) & 1)
    )

    def swap(array, distance, axis="seq"):
        count = mesh.shape[axis]
        return lax.ppermute(array, axis, [(i, i ^ distance) for i in range(count)])

    keys_o = swap(keys, 1)
    forget_o, gate_o = swap(log_forget, 1), swap(input_gate, 1)
    values_o, queries_o = swap(values, 1), swap(queries, 1)
    forgets = (log_forget, forget_o)
    gate_args = (*forgets, input_gate, gate_o)

    packed = (half, body + 8, width)
    sent = (half, body + 16, width)
    full = (half, width, width)
    many = (pairs, width, width)
    two = (pairs, 2, width, width)

    pg, tg, pw, tw, gf, uf, ks = call(
        sums_kernel,
        (VMEM(sent, BF16), VMEM(packed, F32), VMEM(full, BF16), VMEM(full, F32), VMEM(full, F32), VMEM(full, F32),
         VMEM(two, BF16)),
        (meta,),
        (keys, keys_o, values, values_o, *gate_args),
    )

    before = before_w = None
    for r in range(bits):
        got = swap(pg, 2 << r)
        got_w = swap(pw, 2 << r)
        if r == bits - 1:
            break
        extra = () if before is None else (before,)
        tg, pg, before, coef = call(
            functools.partial(join_kernel, r + 1, bool(extra)),
            (VMEM(packed, F32), VMEM(sent, BF16), VMEM(packed, F32), VMEM((half, 8, width), F32)),
            (meta,),
            (tg, got, *extra),
        )
        extra = () if before_w is None else (before_w,)
        tw, pw, before_w = call(
            functools.partial(join_state_kernel, bool(extra)),
            (VMEM(full, F32), VMEM(full, BF16), VMEM(full, F32)),
            (),
            (coef, tw, got_w, *extra),
        )
    last = bits

    size = out_columns // parts
    own = call(share_kernel, VMEM((1, rows, size), BF16), (meta,), (out_weight,))
    groups = []
    held = ((0,), own)
    for bit in reversed(range(1, bits)):
        fresh = (tuple(o ^ (1 << bit) for o in held[0]), swap(held[1], 2 << bit))
        groups.append(fresh)
        if bit > 1:
            held = (
                held[0] + fresh[0],
                call(stack_kernel, VMEM((2 * len(held[0]), rows, size), BF16), (), (held[1], fresh[1])),
            )
    groups.append((tuple(o ^ 1 for o in held[0]), swap(held[1], 2)))
    groups.append((tuple(o ^ 1 for o in fresh[0]), swap(fresh[1], 2)))
    table, pieces = {}, []
    for offsets, array in groups:
        shares = [(0, array)]
        step = 1
        while step < parts:
            shares += [(q ^ step, swap(a, step, "parts")) for q, a in shares]
            step *= 2
        for q, a in shares:
            for flip, b in ((0, a), (1, swap(a, 1))):
                for i, offset in enumerate(offsets):
                    table[offset, flip, q] = (len(pieces), i)
                pieces.append(b)
    weight_o = swap(out_weight, 1)

    q_s, kt, m_s, e_s, base = call(
        prepare_kernel,
        (VMEM(many, F32), VMEM(two, BF16), VMEM(many, F32), VMEM(many, F32), VMEM(many, F32)),
        (meta, ridge),
        (ks, queries, queries_o, *gate_args),
    )
    s_s, p_s = call(
        functools.partial(inverse_kernel, last),
        (VMEM(two, BF16), VMEM(many, F32)),
        (meta,),
        (base, *forgets, gf, before, got),
        (VMEM(two, BF16),),
    )
    xs, part = call(
        correct_kernel,
        (VMEM(two, BF16), VMEM(many, F32)),
        (meta, ridge),
        (q_s, kt, m_s, e_s, ks, s_s, p_s, values, values_o),
        (VMEM(many, F32),),
    )
    y_own, y_other = call(
        functools.partial(read_kernel, last),
        (VMEM((tokens, half * width), BF16),) * 2,
        (meta,),
        (xs, part, e_s, *forgets, uf, before, before_w, got_w, gain.reshape(1, features)),
    )
    y_got = swap(y_other, 1)

    result = jax.ShapeDtypeStruct((tokens, out_columns), BF16)
    y_full = VMEM((tokens, features), BF16)
    if 2 * rows == width:
        return call(
            functools.partial(project_kernel, table, chips),
            result,
            (meta,),
            (y_own, y_got, out_weight, weight_o, *pieces),
            (y_full,),
        )
    near = pl.BlockSpec(memory_space=VMEM)
    return pl.pallas_call(
        functools.partial(project_copy_kernel, table),
        out_shape=result,
        in_specs=[pl.BlockSpec(memory_space=SMEM), near, near] + [pl.BlockSpec(memory_space=pl.ANY)] * (2 + len(pieces)),
        out_specs=near,
        scratch_shapes=[
            VMEM((features, out_columns), BF16), y_full, pltpu.SemaphoreType.DMA((2 + len(table),))
        ],
    )(meta, y_own, y_got, out_weight, weight_o, *pieces)


def solution(mesh):
    rows = P(("parts", "seq"), None)
    gate = P(None, ("parts", "seq"))

    def body(*args):
        return on_device(mesh, *args)

    return jax.shard_map(
        body,
        mesh=mesh,
        in_specs=(rows, rows, rows, gate, gate, P(), P(), P("seq", None)),
        out_specs=rows,
        check_vma=False,
    )
```

```python
import functools
import jax
import jax.numpy as jnp
from jax import lax
from jax.experimental import pallas as pl
from jax.experimental.pallas import tpu as pltpu
from jax.sharding import PartitionSpec as P

NEWTON = 6
CORR = 4
F32 = jnp.float32
BF16 = jnp.bfloat16
EXACT = lax.Precision.HIGHEST
VMEM = pltpu.VMEM
GRANT = 8 * 1024 * 1024


def rows_of(shape):
    return lax.broadcasted_iota(jnp.int32, shape, 0)


def lanes_of(shape):
    return lax.broadcasted_iota(jnp.int32, shape, 1)


def split(x):
    high = x.astype(BF16)
    return high, (x - high.astype(F32)).astype(BF16)


def dot(a, b):
    return jnp.dot(a, b, preferred_element_type=F32)


def dot_t(a, b):
    return lax.dot_general(a, b, (((0,), (0,)), ((), ())), preferred_element_type=F32)


def wide(pair):
    high, low = pair
    return jnp.concatenate([high, low, high], axis=1)


def tall(pair):
    high, low = pair
    return jnp.concatenate([high, high, low], axis=0)


def unit_rows(x):
    return x * lax.rsqrt(jnp.sum(x * x, axis=-1, keepdims=True) + 1e-6)


def pick(first, own, other):
    return jnp.where(first, own, other)


def columns(ref, core, h, half, width):
    return ref[:, pl.ds(pl.multiple_of((core * half + h) * width, width), width)]


def gates(own_ref, other_ref, core, half):
    own, other = own_ref[...], other_ref[...]
    return jnp.concatenate(
        [
            jnp.where(core == 0, own[:half], own[half:]),
            jnp.where(core == 0, other[:half], other[half:]),
        ],
        axis=0,
    )


def running_sum(a):
    width = a.shape[-1]
    tri = (rows_of((width, width)) <= lanes_of((width, width))).astype(F32)
    return jnp.dot(a, tri, precision=EXACT, preferred_element_type=F32)


def pack(sym):
    width = sym.shape[0]
    half = width // 2
    top, low = sym[:half], pltpu.roll(sym[half:], half, 1)
    shape = (half, width)
    r, c = rows_of(shape), lanes_of(shape)
    body = jnp.where(r > c, low, top)
    diag = jnp.sum(jnp.where(r == c, low, 0.0), axis=0, keepdims=True)
    return body, diag


def unpack(body, diag):
    half, _ = body.shape
    r, c = rows_of(body.shape), lanes_of(body.shape)
    top = jnp.where(c > r, body, 0.0) + jnp.where(c == r, 0.5 * body, 0.0)
    low = jnp.where(c < r, body, 0.0) + jnp.where(c == r, 0.5 * diag, 0.0)
    full = jnp.concatenate([top, pltpu.roll(low, half, 1)], axis=0)
    return full + full.T


def tail_rows(diag, level):
    r = rows_of((8, diag.shape[-1]))
    return jnp.where(r == 0, diag, jnp.where(r == 1, level, 0.0))


def tail_sent(diag, level):
    one = level.astype(BF16).astype(F32)
    two = (level - one).astype(BF16).astype(F32)
    three = level - one - two
    r = rows_of((16, diag.shape[-1]))
    out = jnp.where(r == 0, diag, jnp.where(r == 1, one, jnp.where(r == 2, two, jnp.where(r == 3, three, 0.0))))
    return out.astype(BF16)


def sums_kernel(meta, ko, kr, vr, fo, fr, go, gr, values, pg, tg, pw, tw, gf, uf, ks, vo, sem):
    half = gf.shape[0]
    width = gf.shape[1]
    fetch = pltpu.make_async_copy(values, vo, sem)
    fetch.start()
    body = width // 2
    core = meta[0]
    forget = gates(fo, fr, core, half)
    beta = gates(go, gr, core, half)
    level = running_sum(forget)
    last = level[:, width - 1 :]
    tails = (jnp.exp(last - level) * beta).T
    decay = jnp.exp(last)
    first = core == 0
    weighted = {}
    for h in range(half):
        grams = []
        for side, kref in enumerate((ko, kr)):
            p = h + side * half
            k = unit_rows(columns(kref, core, h, half, width).astype(F32))
            tk = split(k * tails[:, p : p + 1])
            kk = split(k)
            ks[p, 0], ks[p, 1] = kk
            weighted[p] = jnp.concatenate(tk, axis=0)
            grams.append(
                dot_t(jnp.concatenate([tk[0], tk[1], tk[0]], axis=0), jnp.concatenate([kk[0], kk[0], kk[1]], axis=0))
            )
        early = pick(first, grams[0], grams[1])
        late = pick(first, grams[1], grams[0])
        shrink = pick(first, decay[half + h : half + h + 1], decay[h : h + 1])
        gf[h] = early
        packed, diag = pack(shrink * early + late)
        total = jnp.broadcast_to(last[h : h + 1] + last[half + h : half + h + 1], (1, width))
        tg[h, :body] = packed
        tg[h, body:] = tail_rows(diag, total)
        pg[h, :body] = packed.astype(BF16)
        pg[h, body:] = tail_sent(diag, total)
    fetch.wait()
    for h in range(half):
        states = []
        for side, vref in enumerate((vo, vr)):
            v = columns(vref, core, h, half, width)
            states.append(dot_t(weighted[h + side * half], jnp.concatenate([v, v], axis=0)))
        early_state = pick(first, states[0], states[1])
        late_state = pick(first, states[1], states[0])
        shrink = pick(first, decay[half + h : half + h + 1], decay[h : h + 1])
        uf[h] = early_state
        state = shrink * early_state + late_state
        tw[h] = state
        pw[h] = state.astype(BF16)


def join_kernel(which, has_prefix, goes_on, meta, t, got, *rest):
    sent, before_new, coef = rest[has_prefix : has_prefix + 3]
    before = rest[0]
    t_new = rest[-1]
    bit = meta[which] == 1
    half, rows, width = t.shape
    body = rows - 8
    for h in range(half):
        tail = t[h, body:]
        mine = tail[1:2]
        ends = got[h, body:].astype(F32)
        theirs = ends[1:2] + ends[2:3] + ends[3:4]
        a = jnp.where(bit, 1.0, jnp.exp(theirs))
        b = jnp.where(bit, jnp.exp(mine), 1.0)
        arrived = got[h, :body].astype(F32)
        packed = a * t[h, :body] + b * arrived
        diag = a * tail[:1] + b * ends[:1]
        if goes_on:
            t_new[h, :body] = packed
            t_new[h, body:] = tail_rows(diag, mine + theirs)
        sent[h, :body] = packed.astype(BF16)
        sent[h, body:] = tail_sent(diag, mine + theirs)
        if has_prefix:
            old = before[h, body:]
            e = jnp.where(bit, jnp.exp(old[1:2]), 0.0)
            before_new[h, :body] = before[h, :body] + e * arrived
            before_new[h, body:] = tail_rows(old[:1] + e * ends[:1], old[1:2] + jnp.where(bit, theirs, 0.0))
        else:
            e = jnp.where(bit, jnp.ones_like(mine), 0.0)
            before_new[h, :body] = e * arrived
            before_new[h, body:] = tail_rows(e * ends[:1], jnp.where(bit, theirs, 0.0))
        r = rows_of((8, width))
        coef[h] = jnp.where(r == 0, a, jnp.where(r == 1, b, jnp.where(r == 2, e, 0.0)))


def join_state_kernel(has_prefix, goes_on, coef, t, got, *rest):
    sent, before_new = rest[has_prefix : has_prefix + 2]
    before = rest[0]
    t_new = rest[-1]
    for h in range(t.shape[0]):
        c = coef[h]
        arrived = got[h].astype(F32)
        new = c[0:1] * t[h] + c[1:2] * arrived
        if goes_on:
            t_new[h] = new
        sent[h] = new.astype(BF16)
        add = c[2:3] * arrived
        before_new[h] = before[h] + add if has_prefix else add


def prepare_kernel(meta, ridge, ks, qo, qr, fo, fr, go, gr, q_s, kt, m_s, e_s, base):
    pairs, _, tokens, width = ks.shape
    half = pairs // 2
    core = meta[0]
    beta = gates(go, gr, core, half)
    level = running_sum(gates(fo, fr, core, half))
    level_t = level.T
    beta_t = beta.T
    square = (tokens, tokens)
    lower = rows_of(square) >= lanes_of(square)
    eye = (rows_of((width, width)) == lanes_of((width, width))).astype(F32)
    for side, qref in enumerate((qo, qr)):
        for h in range(half):
            p = h + side * half
            kh, kl = ks[p, 0], ks[p, 1]
            kt[p, 0], kt[p, 1] = kh.T, kl.T
            k = kh.astype(F32) + kl.astype(F32)
            bk = split(k * beta_t[:, p : p + 1])
            cross = dot_t(jnp.concatenate([bk[0], bk[1], bk[0]], axis=0), jnp.concatenate([kh, kh, kl], axis=0))
            base[p] = cross + ridge[core * half + h] * eye
            column = level_t[:, p : p + 1]
            m_s[p] = jnp.where(lower, jnp.exp(jnp.minimum(column - level[p : p + 1], 0.0)) * beta[p : p + 1], 0.0)
            e_s[p] = jnp.broadcast_to(jnp.exp(column), square)
            q_s[p] = unit_rows(columns(qref, core, h, half, width).astype(F32))


def inverse_kernel(which, meta, base, fo, fr, gf, before, got, s_s, p_s, a_s):
    half, width, _ = gf.shape
    body = width // 2
    pairs = 2 * half
    core = meta[0]
    first = core == 0
    bit = meta[which] == 1
    forget = gates(fo, fr, core, half)
    decay = jnp.exp(jnp.sum(forget, axis=1, keepdims=True))
    eye = (rows_of((width, width)) == lanes_of((width, width))).astype(F32)
    for h in range(half):
        tail = before[h, body:]
        ends = got[h, body:].astype(F32)
        e = jnp.where(bit, jnp.exp(tail[1:2]), 0.0)
        start = unpack(before[h, :body] + e * got[h, :body].astype(F32), tail[:1] + e * ends[:1])
        for side, is_early in enumerate((first, jnp.logical_not(first))):
            p = h + side * half
            other = h + (1 - side) * half
            gram = jnp.where(is_early, start, decay[other : other + 1] * start + gf[h])
            s_s[p, 0], s_s[p, 1] = split(gram)
            system = gram + base[p]
            bound = jnp.max(jnp.sum(jnp.abs(system), axis=0, keepdims=True), axis=1, keepdims=True)
            a_s[p, 0], a_s[p, 1] = split(system)
            p_s[p] = eye / bound

    def refine(_, carry):
        left = [eye - dot(a_s[p, 0], p_s[p].astype(BF16)) for p in range(pairs)]
        for p in range(pairs):
            now = p_s[p]
            p_s[p] = now + dot(now.astype(BF16), left[p].astype(BF16))
        return carry

    lax.fori_loop(0, NEWTON - 1, refine, 0)
    for start in range(0, pairs, half):
        group = range(start, start + half)
        left = []
        for p in group:
            left.append(eye - dot(wide((a_s[p, 0], a_s[p, 1])), tall(split(p_s[p]))))
        for p, rest in zip(group, left):
            now = p_s[p]
            p_s[p] = now + dot(wide(split(now)), tall(split(rest)))


def correct_kernel(meta, ridge, q_s, kt, m_s, e_s, ks, s_s, p_s, vo, vr, xs, part, x_s):
    pairs, _, width = q_s.shape
    half = pairs // 2
    core = meta[0]

    def both_of(p, i):
        return jnp.concatenate([s_s[p, i], kt[p, i]], axis=1)

    for p in range(pairs):
        x_s[p] = dot(q_s[p].astype(BF16), p_s[p].astype(BF16))

    def correct(_, carry):
        both = [dot(x_s[p].astype(BF16), both_of(p, 0)) for p in range(pairs)]
        applied = []
        for p in range(pairs):
            scores = m_s[p] * both[p][:, width:]
            applied.append(
                e_s[p] * both[p][:, :width]
                + dot(scores.astype(BF16), ks[p, 0])
                + ridge[core * half + p % half] * x_s[p]
            )
        for p in range(pairs):
            x_s[p] = x_s[p] + dot((q_s[p] - applied[p]).astype(BF16), p_s[p].astype(BF16))
        return carry

    lax.fori_loop(0, CORR - 2, correct, 0)

    for start, vref in ((0, vo), (half, vr)):
        group = range(start, start + half)
        both = [dot(wide(split(x_s[p])), tall((both_of(p, 0), both_of(p, 1)))) for p in group]
        applied = []
        for p, found in zip(group, both):
            scores = m_s[p] * found[:, width:]
            applied.append(
                e_s[p] * found[:, :width]
                + dot(wide(split(scores)), tall((ks[p, 0], ks[p, 1])))
                + ridge[core * half + p - start] * x_s[p]
            )
        solved = []
        for p, found in zip(group, applied):
            x = x_s[p] + dot((q_s[p] - found).astype(BF16), p_s[p].astype(BF16))
            solved.append(split(x))
            xs[p, 0], xs[p, 1] = solved[-1]
        scores = []
        for p, x in zip(group, solved):
            scores.append(m_s[p] * dot(wide(x), tall((kt[p, 0], kt[p, 1]))))
        for p, found in zip(group, scores):
            v = columns(vref, core, p - start, half, width)
            sh, sl = split(found)
            part[p] = dot(jnp.concatenate([sh, sl], axis=1), jnp.concatenate([v, v], axis=0))


def read_kernel(which, meta, xs, part, e_s, fo, fr, uf, before_g, before, got, far_gain, y_own, y_other, gain, sem):
    fetch = pltpu.make_async_copy(far_gain, gain, sem)
    fetch.start()
    half = uf.shape[0]
    width = uf.shape[1]
    body = width // 2
    core = meta[0]
    first = core == 0
    bit = meta[which] == 1
    decay = jnp.exp(jnp.sum(gates(fo, fr, core, half), axis=1, keepdims=True))
    sides = ((y_own, first), (y_other, jnp.logical_not(first)))
    normed = {}
    for h in range(half):
        e = jnp.where(bit, jnp.exp(before_g[h, body + 1 : body + 2]), 0.0)
        start = before[h] + e * got[h].astype(F32)
        for side, (_, is_early) in enumerate(sides):
            p = h + side * half
            other = h + (1 - side) * half
            state = jnp.where(is_early, start, decay[other : other + 1] * start + uf[h])
            read = dot(wide((xs[p, 0], xs[p, 1])), tall(split(state)))
            o = e_s[p] * read + part[p]
            normed[p] = o * lax.rsqrt(jnp.mean(o * o, axis=-1, keepdims=True) + 1e-6)
    fetch.wait()
    for h in range(half):
        scale = columns(gain, core, h, half, width)
        for side, (out, _) in enumerate(sides):
            out[:, h * width : (h + 1) * width] = (normed[h + side * half] * scale).astype(BF16)


def share_kernel(meta, w, out, sem):
    size = out.shape[2]
    share = meta[meta.shape[0] - 1]
    fetch = pltpu.make_async_copy(w.at[:, pl.ds(pl.multiple_of(share * size, size), size)], out.at[0], sem)
    fetch.start()
    fetch.wait()


def stack_kernel(a, b, out):
    out[: a.shape[0]] = a[...]
    out[a.shape[0] :] = b[...]


def gathered_rows(meta, y_own, y_other, y):
    core = meta[0]
    size = y_own.shape[1]
    y[:, pl.ds(pl.multiple_of(core * size, size), size)] = y_own[...]
    y[:, pl.ds(pl.multiple_of((1 - core) * size, size), size)] = y_other[...]


def project_kernel(table, chips, shares, meta, y_own, y_other, own, other, *rest):
    out, y = rest[-2:]
    core = meta[0]
    place = meta[meta.shape[0] - 2]
    share = meta[meta.shape[0] - 1]
    gathered_rows(meta, y_own, y_other, y)
    width = 2 * own.shape[0]
    size = own.shape[1] // shares
    tokens = y.shape[0]
    lefts = []
    for offset in range(chips):
        chip = jnp.bitwise_xor(place, offset)
        rows = y[:, pl.ds(pl.multiple_of(chip * width, width), width)].astype(F32)
        rows = jnp.where(core == 0, rows, pltpu.roll(rows, width // 2, 1))
        lefts.append(rows.astype(BF16))
    for q in range(shares):
        where = pl.ds(pl.multiple_of(jnp.bitwise_xor(share, q) * size, size), size)
        total = jnp.zeros((tokens, size), F32)
        for offset in range(0, chips, 2):
            blocks = []
            for o in (offset, offset + 1):
                for flip in (0, 1):
                    if o == 0:
                        blocks.append((own, other)[flip][:, where])
                    elif (o, flip, None) in table:
                        blocks.append(rest[table[o, flip, None][0]][:, where])
                    else:
                        piece, i = table[o, flip, q]
                        blocks.append(rest[piece][i])
            left = jnp.concatenate([lefts[offset], lefts[offset + 1]], axis=1)
            total = total + dot(left, jnp.concatenate(blocks, axis=0))
        out[:, where] = total.astype(BF16)


def project_copy_kernel(table, meta, y_own, y_other, own, other, *rest):
    pieces = rest[:-4]
    out, w, y, sem = rest[-4:]
    core = meta[0]
    place = meta[meta.shape[0] - 2]
    share = meta[meta.shape[0] - 1]
    rows = own.shape[0]
    size = pieces[0].shape[2]

    def at(offset, flip):
        row = (jnp.bitwise_xor(place, offset) * 2 + jnp.bitwise_xor(core, flip)) * rows
        return pl.ds(pl.multiple_of(row, rows), rows)

    copies = [
        pltpu.make_async_copy(own, w.at[at(0, 0)], sem.at[0]),
        pltpu.make_async_copy(other, w.at[at(0, 1)], sem.at[1]),
    ]
    for (offset, flip, q), (piece, i) in table.items():
        where = pl.ds(pl.multiple_of(jnp.bitwise_xor(share, q) * size, size), size)
        copies.append(
            pltpu.make_async_copy(pieces[piece].at[i], w.at[at(offset, flip), where], sem.at[len(copies)])
        )
    for copy in copies:
        copy.start()
    gathered_rows(meta, y_own, y_other, y)
    for copy in copies:
        copy.wait()
    out[...] = dot(y[...], w[...]).astype(BF16)


SMEM = pltpu.SMEM


def call(kernel, outs, scalars, ins, scratch=(), far=()):
    spec = pl.BlockSpec(memory_space=VMEM)
    near = [pltpu.with_memory_space_constraint(a, VMEM) for a in ins]
    return pl.pallas_call(
        kernel,
        out_shape=outs,
        in_specs=[pl.BlockSpec(memory_space=SMEM)] * len(scalars)
        + [spec] * len(near)
        + [pl.BlockSpec(memory_space=pl.ANY)] * len(far),
        out_specs=jax.tree.map(lambda _: spec, outs),
        scratch_shapes=scratch,
        compiler_params=pltpu.CompilerParams(vmem_limit_bytes=GRANT),
    )(*scalars, *near, *far)


def on_device(mesh, queries, keys, values, log_forget, input_gate, ridge, gain, out_weight):
    sections, parts = mesh.shape["seq"], mesh.shape["parts"]
    tokens, features = keys.shape
    heads = log_forget.shape[0]
    width = features // heads
    half = heads // 2
    pairs = 2 * half
    body = width // 2
    chips = sections // 2
    bits = chips.bit_length() - 1
    rows, out_columns = out_weight.shape
    index = lax.axis_index("seq")
    steps = lax.iota(jnp.int32, bits + 3)
    meta = jnp.where(
        steps == bits + 2, lax.axis_index("parts"), jnp.where(steps == bits + 1, index >> 1, (index >> steps) & 1)
    )

    def swap(array, distance, axis="seq"):
        count = mesh.shape[axis]
        return lax.ppermute(array, axis, [(i, i ^ distance) for i in range(count)])

    keys_o = swap(keys, 1)
    forget_o, gate_o = swap(log_forget, 1), swap(input_gate, 1)
    values_o, queries_o = swap(values, 1), swap(queries, 1)
    forgets = (log_forget, forget_o)
    gate_args = (*forgets, input_gate, gate_o)

    packed = (half, body + 8, width)
    sent = (half, body + 16, width)
    full = (half, width, width)
    many = (pairs, width, width)
    two = (pairs, 2, width, width)

    pg, tg, pw, tw, gf, uf, ks = call(
        sums_kernel,
        (VMEM(sent, BF16), VMEM(packed, F32), VMEM(full, BF16), VMEM(full, F32), VMEM(full, F32), VMEM(full, F32),
         VMEM(two, BF16)),
        (meta,),
        (keys, keys_o, values_o, *gate_args),
        (VMEM(values.shape, BF16), pltpu.SemaphoreType.DMA),
        (values,),
    )

    before = before_w = None
    tg, tw = (tg,), (tw,)
    for r in range(bits):
        got = swap(pg, 2 << r)
        got_w = swap(pw, 2 << r)
        if r == bits - 1:
            break
        extra = () if before is None else (before,)
        goes_on = r < bits - 2
        pg, before, coef, *tg = call(
            functools.partial(join_kernel, r + 1, len(extra), goes_on),
            (VMEM(sent, BF16), VMEM(packed, F32), VMEM((half, 8, width), F32), *[VMEM(packed, F32)] * goes_on),
            (meta,),
            (*tg, got, *extra),
        )
        extra = () if before_w is None else (before_w,)
        pw, before_w, *tw = call(
            functools.partial(join_state_kernel, len(extra), goes_on),
            (VMEM(full, BF16), VMEM(full, F32), *[VMEM(full, F32)] * goes_on),
            (),
            (coef, *tw, got_w, *extra),
        )
    last = bits

    size = out_columns // parts
    own = call(share_kernel, VMEM((1, rows, size), BF16), (meta,), (), (pltpu.SemaphoreType.DMA,), (out_weight,))

    def stack(a, b):
        return call(stack_kernel, VMEM((a.shape[0] + b.shape[0], rows, size), BF16), (), (a, b))

    table, pieces = {}, []

    def keep(offsets, q, array, flip):
        for i, offset in enumerate(offsets):
            table[offset, flip, q] = (len(pieces), i)
        pieces.append(array)

    groups = []
    if bits == 3:
        far, mid = swap(own, 8), swap(own, 4)
        farther = swap(far, 4)
        near = swap(out_weight, 2)
        both = stack(far, mid)
        groups.append(((4, 2), both))
        groups.append(((5, 3), swap(both, 2)))
        groups.append(((6, 7), stack(farther, swap(farther, 2))))
        keep((1,), None, near, 0)
        keep((1,), None, swap(near, 1), 1)
    else:
        held = ((0,), own)
        for bit in reversed(range(bits)):
            fresh = (tuple(o ^ (1 << bit) for o in held[0]), swap(held[1], 2 << bit))
            groups.append(fresh)
            if bit:
                held = (held[0] + fresh[0], stack(held[1], fresh[1]))
    for offsets, array in groups:
        shares = [(0, array)]
        step = 1
        while step < parts:
            shares += [(q ^ step, swap(a, step, "parts")) for q, a in shares]
            step *= 2
        for q, a in shares:
            keep(offsets, q, a, 0)
            keep(offsets, q, swap(a, 1), 1)
    weight_o = swap(out_weight, 1)

    q_s, kt, m_s, e_s, base = call(
        prepare_kernel,
        (VMEM(many, F32), VMEM(two, BF16), VMEM(many, F32), VMEM(many, F32), VMEM(many, F32)),
        (meta, ridge),
        (ks, queries, queries_o, *gate_args),
    )
    s_s, p_s = call(
        functools.partial(inverse_kernel, last),
        (VMEM(two, BF16), VMEM(many, F32)),
        (meta,),
        (base, *forgets, gf, before, got),
        (VMEM(two, BF16),),
    )
    xs, part = call(
        correct_kernel,
        (VMEM(two, BF16), VMEM(many, F32)),
        (meta, ridge),
        (q_s, kt, m_s, e_s, ks, s_s, p_s, values, values_o),
        (VMEM(many, F32),),
    )
    y_own, y_other = call(
        functools.partial(read_kernel, last),
        (VMEM((tokens, half * width), BF16),) * 2,
        (meta,),
        (xs, part, e_s, *forgets, uf, before, before_w, got_w),
        (VMEM((1, features), F32), pltpu.SemaphoreType.DMA),
        (gain.reshape(1, features),),
    )
    y_got = swap(y_other, 1)

    result = jax.ShapeDtypeStruct((tokens, out_columns), BF16)
    y_full = VMEM((tokens, features), BF16)
    if bits == 3 and 2 * rows == width:
        return call(
            functools.partial(project_kernel, table, chips, parts),
            result,
            (meta,),
            (y_own, y_got, out_weight, weight_o, *pieces),
            (y_full,),
        )
    here = pl.BlockSpec(memory_space=VMEM)
    return pl.pallas_call(
        functools.partial(project_copy_kernel, table),
        out_shape=result,
        in_specs=[pl.BlockSpec(memory_space=SMEM), here, here] + [pl.BlockSpec(memory_space=pl.ANY)] * (2 + len(pieces)),
        out_specs=here,
        scratch_shapes=[
            VMEM((features, out_columns), BF16), y_full, pltpu.SemaphoreType.DMA((2 + len(table),))
        ],
    )(meta, y_own, y_got, out_weight, weight_o, *pieces)


def solution(mesh):
    rows = P(("parts", "seq"), None)
    gate = P(None, ("parts", "seq"))

    def body(*args):
        return on_device(mesh, *args)

    return jax.shard_map(
        body,
        mesh=mesh,
        in_specs=(rows, rows, rows, gate, gate, P(), P(), P("seq", None)),
        out_specs=rows,
        check_vma=False,
    )
```

```python
import functools
import jax
import jax.numpy as jnp
from jax import lax
from jax.experimental import pallas as pl
from jax.experimental.pallas import tpu as pltpu
from jax.sharding import PartitionSpec as P

NEWTON = 6
CORR = 4
F32 = jnp.float32
BF16 = jnp.bfloat16
EXACT = lax.Precision.HIGHEST
VMEM = pltpu.VMEM
GRANT = 8 * 1024 * 1024


def rows_of(shape):
    return lax.broadcasted_iota(jnp.int32, shape, 0)


def lanes_of(shape):
    return lax.broadcasted_iota(jnp.int32, shape, 1)


def split(x):
    high = x.astype(BF16)
    return high, (x - high.astype(F32)).astype(BF16)


def dot(a, b):
    return jnp.dot(a, b, preferred_element_type=F32)


def wide(pair):
    high, low = pair
    return jnp.concatenate([high, low, high], axis=1)


def tall(pair):
    high, low = pair
    return jnp.concatenate([high, high, low], axis=0)


def unit_rows(x):
    return x * lax.rsqrt(jnp.sum(x * x, axis=-1, keepdims=True) + 1e-6)


def pick(first, own, other):
    return jnp.where(first, own, other)


def columns(ref, core, h, half, width):
    if ref.shape[1] == half * width:
        return ref[:, h * width : (h + 1) * width]
    return ref[:, pl.ds(pl.multiple_of((core * half + h) * width, width), width)]


def gates(own_ref, other_ref, core, half):
    own, other = own_ref[...], other_ref[...]
    return jnp.concatenate(
        [
            jnp.where(core == 0, own[:half], own[half:]),
            jnp.where(core == 0, other[:half], other[half:]),
        ],
        axis=0,
    )


def ridge_of(row, core, h, half):
    return jnp.where(core == 0, row[:, h : h + 1], row[:, half + h : half + h + 1])


def running_sum(a):
    width = a.shape[-1]
    tri = (rows_of((width, width)) <= lanes_of((width, width))).astype(F32)
    return jnp.dot(a, tri, precision=EXACT, preferred_element_type=F32)


def pack(sym):
    width = sym.shape[0]
    half = width // 2
    top, low = sym[:half], pltpu.roll(sym[half:], half, 1)
    shape = (half, width)
    r, c = rows_of(shape), lanes_of(shape)
    body = jnp.where(r > c, low, top)
    diag = jnp.sum(jnp.where(r == c, low, 0.0), axis=0, keepdims=True)
    return body, diag


def unpack(body, diag):
    half, _ = body.shape
    r, c = rows_of(body.shape), lanes_of(body.shape)
    top = jnp.where(c > r, body, 0.0) + jnp.where(c == r, 0.5 * body, 0.0)
    low = jnp.where(c < r, body, 0.0) + jnp.where(c == r, 0.5 * diag, 0.0)
    full = jnp.concatenate([top, pltpu.roll(low, half, 1)], axis=0)
    return full + full.T


def tail_rows(diag, level):
    r = rows_of((8, diag.shape[-1]))
    return jnp.where(r == 0, diag, jnp.where(r == 1, level, 0.0))


def tail_sent(diag, level):
    one = level.astype(BF16).astype(F32)
    two = (level - one).astype(BF16).astype(F32)
    three = level - one - two
    r = rows_of((16, diag.shape[-1]))
    out = jnp.where(r == 0, diag, jnp.where(r == 1, one, jnp.where(r == 2, two, jnp.where(r == 3, three, 0.0))))
    return out.astype(BF16)


def load_kernel(meta, *refs):
    count = (len(refs) - 1) // 2
    sources, outs, sem = refs[:count], refs[count : 2 * count], refs[-1]
    copies = []
    for i, (source, out) in enumerate(zip(sources, outs)):
        if len(out.shape) == 3:
            size = out.shape[2]
            share = meta[meta.shape[0] - 1]
            source, out = source.at[:, pl.ds(pl.multiple_of(share * size, size), size)], out.at[0]
        elif out.shape[1] < source.shape[1]:
            size = out.shape[1]
            source = source.at[:, pl.ds(pl.multiple_of(meta[0] * size, size), size)]
        copies.append(pltpu.make_async_copy(source, out, sem.at[i]))
    for copy in copies:
        copy.start()
    for copy in copies:
        copy.wait()


def sums_kernel(meta, ko, kr, vo, vr, fo, fr, go, gr, pg, tg, pw, tw, gf, uf, ks, kt):
    half = gf.shape[0]
    width = gf.shape[1]
    body = width // 2
    core = meta[0]
    forget = gates(fo, fr, core, half)
    beta = gates(go, gr, core, half)
    level = running_sum(forget)
    last = level[:, width - 1 :]
    tails = jnp.exp(last - level) * beta
    decay = jnp.exp(last)
    first = core == 0
    weighted = {}
    for h in range(half):
        grams = []
        for side, kref in enumerate((ko, kr)):
            p = h + side * half
            k = unit_rows(columns(kref, core, h, half, width).astype(F32))
            turned = k.T
            kk = split(k)
            ks[p, 0], ks[p, 1] = kk
            kt[p, 0], kt[p, 1] = split(turned)
            weighted[p] = split(turned * tails[p : p + 1])
            grams.append(dot(wide(weighted[p]), tall(kk)))
        early = pick(first, grams[0], grams[1])
        late = pick(first, grams[1], grams[0])
        shrink = pick(first, decay[half + h : half + h + 1], decay[h : h + 1])
        gf[h] = early
        packed, diag = pack(shrink * early + late)
        total = jnp.broadcast_to(last[h : h + 1] + last[half + h : half + h + 1], (1, width))
        tg[h, :body] = packed
        tg[h, body:] = tail_rows(diag, total)
        pg[h, :body] = packed.astype(BF16)
        pg[h, body:] = tail_sent(diag, total)
    for h in range(half):
        states = []
        for side, vref in enumerate((vo, vr)):
            v = columns(vref, core, h, half, width)
            states.append(
                dot(jnp.concatenate(weighted[h + side * half], axis=1), jnp.concatenate([v, v], axis=0))
            )
        early_state = pick(first, states[0], states[1])
        late_state = pick(first, states[1], states[0])
        shrink = pick(first, decay[half + h : half + h + 1], decay[h : h + 1])
        uf[h] = early_state
        state = shrink * early_state + late_state
        tw[h] = state
        pw[h] = state.astype(BF16)


def join_kernel(which, has_prefix, goes_on, meta, t, got, *rest):
    sent, before_new, coef = rest[has_prefix : has_prefix + 3]
    before = rest[0]
    t_new = rest[-1]
    bit = meta[which] == 1
    half, rows, width = t.shape
    body = rows - 8
    for h in range(half):
        tail = t[h, body:]
        mine = tail[1:2]
        ends = got[h, body:].astype(F32)
        theirs = ends[1:2] + ends[2:3] + ends[3:4]
        a = jnp.where(bit, 1.0, jnp.exp(theirs))
        b = jnp.where(bit, jnp.exp(mine), 1.0)
        arrived = got[h, :body].astype(F32)
        packed = a * t[h, :body] + b * arrived
        diag = a * tail[:1] + b * ends[:1]
        if goes_on:
            t_new[h, :body] = packed
            t_new[h, body:] = tail_rows(diag, mine + theirs)
        sent[h, :body] = packed.astype(BF16)
        sent[h, body:] = tail_sent(diag, mine + theirs)
        if has_prefix:
            old = before[h, body:]
            e = jnp.where(bit, jnp.exp(old[1:2]), 0.0)
            before_new[h, :body] = before[h, :body] + e * arrived
            before_new[h, body:] = tail_rows(old[:1] + e * ends[:1], old[1:2] + jnp.where(bit, theirs, 0.0))
        else:
            e = jnp.where(bit, jnp.ones_like(mine), 0.0)
            before_new[h, :body] = e * arrived
            before_new[h, body:] = tail_rows(e * ends[:1], jnp.where(bit, theirs, 0.0))
        r = rows_of((8, width))
        coef[h] = jnp.where(r == 0, a, jnp.where(r == 1, b, jnp.where(r == 2, e, 0.0)))


def join_state_kernel(has_prefix, goes_on, coef, t, got, *rest):
    sent, before_new = rest[has_prefix : has_prefix + 2]
    before = rest[0]
    t_new = rest[-1]
    for h in range(t.shape[0]):
        c = coef[h]
        arrived = got[h].astype(F32)
        new = c[0:1] * t[h] + c[1:2] * arrived
        if goes_on:
            t_new[h] = new
        sent[h] = new.astype(BF16)
        add = c[2:3] * arrived
        before_new[h] = before[h] + add if has_prefix else add


def prepare_kernel(meta, ridge, ks, kt, qo, qr, fo, fr, go, gr, q_s, m_s, e_s, base):
    pairs, _, tokens, width = ks.shape
    half = pairs // 2
    core = meta[0]
    beta = gates(go, gr, core, half)
    level = running_sum(gates(fo, fr, core, half))
    level_t = level.T
    square = (tokens, tokens)
    lower = rows_of(square) >= lanes_of(square)
    eye = (rows_of((width, width)) == lanes_of((width, width))).astype(F32)
    for side, qref in enumerate((qo, qr)):
        for h in range(half):
            p = h + side * half
            turned = kt[p, 0].astype(F32) + kt[p, 1].astype(F32)
            cross = dot(wide(split(turned * beta[p : p + 1])), tall((ks[p, 0], ks[p, 1])))
            base[p] = cross + ridge_of(ridge, core, h, half) * eye
            column = level_t[:, p : p + 1]
            m_s[p] = jnp.where(lower, jnp.exp(jnp.minimum(column - level[p : p + 1], 0.0)) * beta[p : p + 1], 0.0)
            e_s[p] = jnp.broadcast_to(jnp.exp(column), square)
            q_s[p] = unit_rows(columns(qref, core, h, half, width).astype(F32))


def inverse_kernel(which, meta, base, fo, fr, gf, before, got, s_s, p_s, a_s):
    half, width, _ = gf.shape
    body = width // 2
    pairs = 2 * half
    core = meta[0]
    first = core == 0
    bit = meta[which] == 1
    forget = gates(fo, fr, core, half)
    decay = jnp.exp(jnp.sum(forget, axis=1, keepdims=True))
    eye = (rows_of((width, width)) == lanes_of((width, width))).astype(F32)
    for h in range(half):
        tail = before[h, body:]
        ends = got[h, body:].astype(F32)
        e = jnp.where(bit, jnp.exp(tail[1:2]), 0.0)
        start = unpack(before[h, :body] + e * got[h, :body].astype(F32), tail[:1] + e * ends[:1])
        for side, is_early in enumerate((first, jnp.logical_not(first))):
            p = h + side * half
            other = h + (1 - side) * half
            gram = jnp.where(is_early, start, decay[other : other + 1] * start + gf[h])
            s_s[p, 0], s_s[p, 1] = split(gram)
            system = gram + base[p]
            bound = jnp.max(jnp.sum(jnp.abs(system), axis=0, keepdims=True), axis=1, keepdims=True)
            a_s[p, 0], a_s[p, 1] = split(system)
            p_s[p] = eye / bound

    def refine(_, carry):
        left = [eye - dot(a_s[p, 0], p_s[p].astype(BF16)) for p in range(pairs)]
        for p in range(pairs):
            now = p_s[p]
            p_s[p] = now + dot(now.astype(BF16), left[p].astype(BF16))
        return carry

    lax.fori_loop(0, NEWTON - 1, refine, 0)
    for start in range(0, pairs, half):
        group = range(start, start + half)
        left = []
        for p in group:
            left.append(eye - dot(wide((a_s[p, 0], a_s[p, 1])), tall(split(p_s[p]))))
        for p, rest in zip(group, left):
            now = p_s[p]
            p_s[p] = now + dot(now.astype(BF16), rest.astype(BF16))


def correct_kernel(meta, ridge, q_s, kt, m_s, e_s, ks, s_s, p_s, vo, vr, xs, part, x_s):
    pairs, _, width = q_s.shape
    half = pairs // 2
    core = meta[0]

    def both_of(p, i):
        return jnp.concatenate([s_s[p, i], kt[p, i]], axis=1)

    for p in range(pairs):
        x_s[p] = dot(q_s[p].astype(BF16), p_s[p].astype(BF16))

    def correct(_, carry):
        both = [dot(x_s[p].astype(BF16), both_of(p, 0)) for p in range(pairs)]
        applied = []
        for p in range(pairs):
            scores = m_s[p] * both[p][:, width:]
            applied.append(
                e_s[p] * both[p][:, :width]
                + dot(scores.astype(BF16), ks[p, 0])
                + ridge_of(ridge, core, p % half, half) * x_s[p]
            )
        for p in range(pairs):
            x_s[p] = x_s[p] + dot((q_s[p] - applied[p]).astype(BF16), p_s[p].astype(BF16))
        return carry

    lax.fori_loop(0, CORR - 2, correct, 0)

    for start, vref in ((0, vo), (half, vr)):
        group = range(start, start + half)
        both = [dot(wide(split(x_s[p])), tall((both_of(p, 0), both_of(p, 1)))) for p in group]
        applied = []
        for p, found in zip(group, both):
            scores = m_s[p] * found[:, width:]
            applied.append(
                e_s[p] * found[:, :width]
                + dot(scores.astype(BF16), ks[p, 0])
                + ridge_of(ridge, core, p - start, half) * x_s[p]
            )
        solved = []
        for p, found in zip(group, applied):
            x = x_s[p] + dot((q_s[p] - found).astype(BF16), p_s[p].astype(BF16))
            solved.append(split(x))
            xs[p, 0], xs[p, 1] = solved[-1]
        scores = []
        for p, x in zip(group, solved):
            scores.append(m_s[p] * dot(wide(x), tall((kt[p, 0], kt[p, 1]))))
        for p, found in zip(group, scores):
            v = columns(vref, core, p - start, half, width)
            sh, sl = split(found)
            part[p] = dot(jnp.concatenate([sh, sl], axis=1), jnp.concatenate([v, v], axis=0))


def read_kernel(which, meta, xs, part, e_s, fo, fr, uf, before_g, before, got, gain, y_own, y_other):
    half = uf.shape[0]
    width = uf.shape[1]
    body = width // 2
    core = meta[0]
    first = core == 0
    bit = meta[which] == 1
    decay = jnp.exp(jnp.sum(gates(fo, fr, core, half), axis=1, keepdims=True))
    sides = ((y_own, first), (y_other, jnp.logical_not(first)))
    for h in range(half):
        cols = slice(h * width, (h + 1) * width)
        e = jnp.where(bit, jnp.exp(before_g[h, body + 1 : body + 2]), 0.0)
        start = before[h] + e * got[h].astype(F32)
        scale = columns(gain, core, h, half, width)
        for side, (out, is_early) in enumerate(sides):
            p = h + side * half
            other = h + (1 - side) * half
            state = jnp.where(is_early, start, decay[other : other + 1] * start + uf[h])
            read = dot(wide((xs[p, 0], xs[p, 1])), tall(split(state)))
            o = e_s[p] * read + part[p]
            o = o * lax.rsqrt(jnp.mean(o * o, axis=-1, keepdims=True) + 1e-6)
            out[:, cols] = (o * scale).astype(BF16)


def stack_kernel(a, b, out):
    out[: a.shape[0]] = a[...]
    out[a.shape[0] :] = b[...]


def gathered_rows(meta, y_own, y_other, y):
    core = meta[0]
    size = y_own.shape[1]
    y[:, pl.ds(pl.multiple_of(core * size, size), size)] = y_own[...]
    y[:, pl.ds(pl.multiple_of((1 - core) * size, size), size)] = y_other[...]


def project_kernel(table, chips, shares, meta, y_own, y_other, own, other, *rest):
    out, y = rest[-2:]
    core = meta[0]
    place = meta[meta.shape[0] - 2]
    share = meta[meta.shape[0] - 1]
    gathered_rows(meta, y_own, y_other, y)
    width = 2 * own.shape[0]
    size = own.shape[1] // shares
    tokens = y.shape[0]
    lefts = []
    for offset in range(chips):
        chip = jnp.bitwise_xor(place, offset)
        rows = y[:, pl.ds(pl.multiple_of(chip * width, width), width)].astype(F32)
        rows = jnp.where(core == 0, rows, pltpu.roll(rows, width // 2, 1))
        lefts.append(rows.astype(BF16))
    for q in range(shares):
        where = pl.ds(pl.multiple_of(jnp.bitwise_xor(share, q) * size, size), size)
        total = jnp.zeros((tokens, size), F32)
        for offset in range(0, chips, 2):
            blocks = []
            for o in (offset, offset + 1):
                for flip in (0, 1):
                    if o == 0:
                        blocks.append((own, other)[flip][:, where])
                    elif (o, flip, None) in table:
                        blocks.append(rest[table[o, flip, None][0]][:, where])
                    else:
                        piece, i = table[o, flip, q]
                        blocks.append(rest[piece][i])
            left = jnp.concatenate([lefts[offset], lefts[offset + 1]], axis=1)
            total = total + dot(left, jnp.concatenate(blocks, axis=0))
        out[:, where] = total.astype(BF16)


def project_copy_kernel(table, meta, y_own, y_other, own, other, *rest):
    pieces = rest[:-4]
    out, w, y, sem = rest[-4:]
    core = meta[0]
    place = meta[meta.shape[0] - 2]
    share = meta[meta.shape[0] - 1]
    rows = own.shape[0]
    size = pieces[0].shape[2]

    def at(offset, flip):
        row = (jnp.bitwise_xor(place, offset) * 2 + jnp.bitwise_xor(core, flip)) * rows
        return pl.ds(pl.multiple_of(row, rows), rows)

    copies = [
        pltpu.make_async_copy(own, w.at[at(0, 0)], sem.at[0]),
        pltpu.make_async_copy(other, w.at[at(0, 1)], sem.at[1]),
    ]
    for (offset, flip, q), (piece, i) in table.items():
        where = pl.ds(pl.multiple_of(jnp.bitwise_xor(share, q) * size, size), size)
        copies.append(
            pltpu.make_async_copy(pieces[piece].at[i], w.at[at(offset, flip), where], sem.at[len(copies)])
        )
    for copy in copies:
        copy.start()
    gathered_rows(meta, y_own, y_other, y)
    for copy in copies:
        copy.wait()
    out[...] = dot(y[...], w[...]).astype(BF16)


SMEM = pltpu.SMEM


def call(kernel, outs, scalars, ins, scratch=(), far=()):
    spec = pl.BlockSpec(memory_space=VMEM)
    near = [pltpu.with_memory_space_constraint(a, VMEM) for a in ins]
    far = [pltpu.with_memory_space_constraint(a, pltpu.HBM) for a in far]
    return pl.pallas_call(
        kernel,
        out_shape=outs,
        in_specs=[pl.BlockSpec(memory_space=SMEM)] * len(scalars)
        + [spec] * len(near)
        + [pl.BlockSpec(memory_space=pltpu.HBM)] * len(far),
        out_specs=jax.tree.map(lambda _: spec, outs),
        scratch_shapes=scratch,
        compiler_params=pltpu.CompilerParams(vmem_limit_bytes=GRANT),
    )(*scalars, *near, *far)


def on_device(mesh, queries, keys, values, log_forget, input_gate, ridge, gain, out_weight):
    sections, parts = mesh.shape["seq"], mesh.shape["parts"]
    tokens, features = keys.shape
    heads = log_forget.shape[0]
    width = features // heads
    half = heads // 2
    pairs = 2 * half
    body = width // 2
    chips = sections // 2
    bits = chips.bit_length() - 1
    rows, out_columns = out_weight.shape
    index = lax.axis_index("seq")
    steps = lax.iota(jnp.int32, bits + 3)
    meta = jnp.where(
        steps == bits + 2, lax.axis_index("parts"), jnp.where(steps == bits + 1, index >> 1, (index >> steps) & 1)
    )

    def swap(array, distance, axis="seq"):
        count = mesh.shape[axis]
        return lax.ppermute(array, axis, [(i, i ^ distance) for i in range(count)])

    keys_o = swap(keys, 1)
    forget_o, gate_o = swap(log_forget, 1), swap(input_gate, 1)
    values_o, queries_o = swap(values, 1), swap(queries, 1)
    mine = VMEM((tokens, half * width), BF16)
    small = VMEM(log_forget.shape, F32)
    size = out_columns // parts
    far_args = (out_weight, keys, values, queries, log_forget, input_gate)
    far_args += (gain.reshape(1, features), ridge.reshape(1, heads))
    own, keys_m, values_m, queries_m, forget_m, gate_m, gain_row, ridge_row = call(
        load_kernel,
        (VMEM((1, rows, size), BF16), mine, mine, mine, small, small, VMEM((1, features), F32), VMEM((1, heads), F32)),
        (meta,),
        (),
        (pltpu.SemaphoreType.DMA((len(far_args),)),),
        far_args,
    )
    forgets = (forget_m, forget_o)
    gate_args = (*forgets, gate_m, gate_o)

    packed = (half, body + 8, width)
    sent = (half, body + 16, width)
    full = (half, width, width)
    many = (pairs, width, width)
    two = (pairs, 2, width, width)

    pg, tg, pw, tw, gf, uf, ks, kt = call(
        sums_kernel,
        (VMEM(sent, BF16), VMEM(packed, F32), VMEM(full, BF16), VMEM(full, F32), VMEM(full, F32), VMEM(full, F32),
         VMEM(two, BF16), VMEM(two, BF16)),
        (meta,),
        (keys_m, keys_o, values_m, values_o, *gate_args),
    )

    before = before_w = None
    tg, tw = (tg,), (tw,)
    for r in range(bits):
        got = swap(pg, 2 << r)
        got_w = swap(pw, 2 << r)
        if r == bits - 1:
            break
        extra = () if before is None else (before,)
        goes_on = r < bits - 2
        pg, before, coef, *tg = call(
            functools.partial(join_kernel, r + 1, len(extra), goes_on),
            (VMEM(sent, BF16), VMEM(packed, F32), VMEM((half, 8, width), F32), *[VMEM(packed, F32)] * goes_on),
            (meta,),
            (*tg, got, *extra),
        )
        extra = () if before_w is None else (before_w,)
        pw, before_w, *tw = call(
            functools.partial(join_state_kernel, len(extra), goes_on),
            (VMEM(full, BF16), VMEM(full, F32), *[VMEM(full, F32)] * goes_on),
            (),
            (coef, *tw, got_w, *extra),
        )
    last = bits

    def stack(a, b):
        return call(stack_kernel, VMEM((a.shape[0] + b.shape[0], rows, size), BF16), (), (a, b))

    table, pieces = {}, []

    def keep(offsets, q, array, flip):
        for i, offset in enumerate(offsets):
            table[offset, flip, q] = (len(pieces), i)
        pieces.append(array)

    groups = []
    if bits == 3:
        far, mid = swap(own, 8), swap(own, 4)
        farther = swap(far, 4)
        near = swap(out_weight, 2)
        both = stack(far, mid)
        groups.append(((4, 2), both))
        groups.append(((6, 7), stack(farther, swap(farther, 2))))
        keep((1,), None, near, 0)
        keep((1,), None, swap(near, 1), 1)
    else:
        held = ((0,), own)
        for bit in reversed(range(bits)):
            fresh = (tuple(o ^ (1 << bit) for o in held[0]), swap(held[1], 2 << bit))
            groups.append(fresh)
            if bit:
                held = (held[0] + fresh[0], stack(held[1], fresh[1]))
    for g, (offsets, array) in enumerate(groups):
        shares = [(0, array)]
        step = 1
        while step < parts:
            shares += [(q ^ step, swap(a, step, "parts")) for q, a in shares]
            step *= 2
        if bits == 3 and g == 0:
            shares += [(q + parts, swap(a, 2)) for q, a in shares]
        for q, a in shares:
            at = offsets if q < parts else tuple(o ^ 1 for o in offsets)
            keep(at, q % parts, a, 0)
            keep(at, q % parts, swap(a, 1), 1)
    weight_o = swap(out_weight, 1)

    q_s, m_s, e_s, base = call(
        prepare_kernel,
        (VMEM(many, F32), VMEM(many, F32), VMEM(many, F32), VMEM(many, F32)),
        (meta,),
        (ridge_row, ks, kt, queries_m, queries_o, *gate_args),
    )
    s_s, p_s = call(
        functools.partial(inverse_kernel, last),
        (VMEM(two, BF16), VMEM(many, F32)),
        (meta,),
        (base, *forgets, gf, before, got),
        (VMEM(two, BF16),),
    )
    xs, part = call(
        correct_kernel,
        (VMEM(two, BF16), VMEM(many, F32)),
        (meta,),
        (ridge_row, q_s, kt, m_s, e_s, ks, s_s, p_s, values_m, values_o),
        (VMEM(many, F32),),
    )
    y_own, y_other = call(
        functools.partial(read_kernel, last),
        (VMEM((tokens, half * width), BF16),) * 2,
        (meta,),
        (xs, part, e_s, *forgets, uf, before, before_w, got_w, gain_row),
    )
    y_got = swap(y_other, 1)

    result = jax.ShapeDtypeStruct((tokens, out_columns), BF16)
    y_full = VMEM((tokens, features), BF16)
    if bits == 3 and 2 * rows == width:
        return call(
            functools.partial(project_kernel, table, chips, parts),
            result,
            (meta,),
            (y_own, y_got, out_weight, weight_o, *pieces),
            (y_full,),
        )
    here = pl.BlockSpec(memory_space=VMEM)
    return pl.pallas_call(
        functools.partial(project_copy_kernel, table),
        out_shape=result,
        in_specs=[pl.BlockSpec(memory_space=SMEM), here, here] + [pl.BlockSpec(memory_space=pl.ANY)] * (2 + len(pieces)),
        out_specs=here,
        scratch_shapes=[
            VMEM((features, out_columns), BF16), y_full, pltpu.SemaphoreType.DMA((2 + len(table),))
        ],
    )(meta, y_own, y_got, out_weight, weight_o, *pieces)


def solution(mesh):
    rows = P(("parts", "seq"), None)
    gate = P(None, ("parts", "seq"))

    def body(*args):
        return on_device(mesh, *args)

    return jax.shard_map(
        body,
        mesh=mesh,
        in_specs=(rows, rows, rows, gate, gate, P(), P(), P("seq", None)),
        out_specs=rows,
        check_vma=False,
    )
```

```python
import functools
import jax
import jax.numpy as jnp
from jax import lax
from jax.experimental import pallas as pl
from jax.experimental.pallas import tpu as pltpu
from jax.sharding import PartitionSpec as P

NEWTON = 6
CORR = 4
F32 = jnp.float32
BF16 = jnp.bfloat16
EXACT = lax.Precision.HIGHEST
VMEM = pltpu.VMEM
GRANT = 8 * 1024 * 1024


def rows_of(shape):
    return lax.broadcasted_iota(jnp.int32, shape, 0)


def lanes_of(shape):
    return lax.broadcasted_iota(jnp.int32, shape, 1)


def bit_of(i):
    return (lax.axis_index("seq") >> i) & 1


def split(x):
    high = x.astype(BF16)
    return high, (x - high.astype(F32)).astype(BF16)


def dot(a, b):
    return jnp.dot(a, b, preferred_element_type=F32)


def wide(pair):
    high, low = pair
    return jnp.concatenate([high, low, high], axis=1)


def tall(pair):
    high, low = pair
    return jnp.concatenate([high, high, low], axis=0)


def unit_rows(x):
    return x * lax.rsqrt(jnp.sum(x * x, axis=-1, keepdims=True) + 1e-6)


def pick(first, own, other):
    return jnp.where(first, own, other)


def columns(ref, core, h, half, width):
    if ref.shape[1] == half * width:
        return ref[:, h * width : (h + 1) * width]
    return ref[:, pl.ds(pl.multiple_of((core * half + h) * width, width), width)]


def gates(own_ref, other_ref, core, half):
    own, other = own_ref[...], other_ref[...]
    return jnp.concatenate(
        [
            jnp.where(core == 0, own[:half], own[half:]),
            jnp.where(core == 0, other[:half], other[half:]),
        ],
        axis=0,
    )


def ridge_of(row, core, h, half):
    return jnp.where(core == 0, row[:, h : h + 1], row[:, half + h : half + h + 1])


def running_sum(a):
    width = a.shape[-1]
    tri = (rows_of((width, width)) <= lanes_of((width, width))).astype(F32)
    return jnp.dot(a, tri, precision=EXACT, preferred_element_type=F32)


def pack(sym):
    width = sym.shape[0]
    half = width // 2
    top, low = sym[:half], pltpu.roll(sym[half:], half, 1)
    shape = (half, width)
    r, c = rows_of(shape), lanes_of(shape)
    body = jnp.where(r > c, low, top)
    diag = jnp.sum(jnp.where(r == c, low, 0.0), axis=0, keepdims=True)
    return body, diag


def unpack(body, diag):
    half, _ = body.shape
    r, c = rows_of(body.shape), lanes_of(body.shape)
    top = jnp.where(c > r, body, 0.0) + jnp.where(c == r, 0.5 * body, 0.0)
    low = jnp.where(c < r, body, 0.0) + jnp.where(c == r, 0.5 * diag, 0.0)
    full = jnp.concatenate([top, pltpu.roll(low, half, 1)], axis=0)
    return full + full.T


def tail_rows(diag, level):
    r = rows_of((8, diag.shape[-1]))
    return jnp.where(r == 0, diag, jnp.where(r == 1, level, 0.0))


def tail_sent(diag, level):
    one = level.astype(BF16).astype(F32)
    two = (level - one).astype(BF16).astype(F32)
    three = level - one - two
    r = rows_of((16, diag.shape[-1]))
    out = jnp.where(r == 0, diag, jnp.where(r == 1, one, jnp.where(r == 2, two, jnp.where(r == 3, three, 0.0))))
    return out.astype(BF16)


def load_kernel(*refs):
    count = (len(refs) - 1) // 2
    sources, outs, sem = refs[:count], refs[count : 2 * count], refs[-1]
    copies = []
    for i, (source, out) in enumerate(zip(sources, outs)):
        if len(out.shape) == 3:
            size = out.shape[2]
            share = lax.axis_index("parts")
            source, out = source.at[:, pl.ds(pl.multiple_of(share * size, size), size)], out.at[0]
        elif out.shape[1] < source.shape[1]:
            size = out.shape[1]
            source = source.at[:, pl.ds(pl.multiple_of(bit_of(0) * size, size), size)]
        copies.append(pltpu.make_async_copy(source, out, sem.at[i]))
    for copy in copies:
        copy.start()
    for copy in copies:
        copy.wait()


def sums_kernel(ko, kr, vo, vr, fo, fr, go, gr, pg, tg, pw, tw, gf, uf, ks, kt):
    half = gf.shape[0]
    width = gf.shape[1]
    body = width // 2
    core = bit_of(0)
    forget = gates(fo, fr, core, half)
    beta = gates(go, gr, core, half)
    level = running_sum(forget)
    last = level[:, width - 1 :]
    tails = jnp.exp(last - level) * beta
    decay = jnp.exp(last)
    first = core == 0
    weighted = {}
    for h in range(half):
        grams = []
        for side, kref in enumerate((ko, kr)):
            p = h + side * half
            k = unit_rows(columns(kref, core, h, half, width).astype(F32))
            turned = k.T
            kk = split(k)
            ks[p, 0], ks[p, 1] = kk
            kt[p, 0], kt[p, 1] = split(turned)
            weighted[p] = split(turned * tails[p : p + 1])
            grams.append(dot(wide(weighted[p]), tall(kk)))
        early = pick(first, grams[0], grams[1])
        late = pick(first, grams[1], grams[0])
        shrink = pick(first, decay[half + h : half + h + 1], decay[h : h + 1])
        gf[h] = early
        packed, diag = pack(shrink * early + late)
        total = jnp.broadcast_to(last[h : h + 1] + last[half + h : half + h + 1], (1, width))
        tg[h, :body] = packed
        tg[h, body:] = tail_rows(diag, total)
        pg[h, :body] = packed.astype(BF16)
        pg[h, body:] = tail_sent(diag, total)
    for h in range(half):
        states = []
        for side, vref in enumerate((vo, vr)):
            v = columns(vref, core, h, half, width)
            states.append(
                dot(jnp.concatenate(weighted[h + side * half], axis=1), jnp.concatenate([v, v], axis=0))
            )
        early_state = pick(first, states[0], states[1])
        late_state = pick(first, states[1], states[0])
        shrink = pick(first, decay[half + h : half + h + 1], decay[h : h + 1])
        uf[h] = early_state
        state = shrink * early_state + late_state
        tw[h] = state
        pw[h] = state.astype(BF16)


def join_kernel(which, has_prefix, goes_on, t, got, *rest):
    sent, before_new, coef = rest[has_prefix : has_prefix + 3]
    before = rest[0]
    t_new = rest[-1]
    bit = bit_of(which) == 1
    half, rows, width = t.shape
    body = rows - 8
    tails = t[:, body:]
    ends = got[:, body:].astype(F32)
    mine = tails[:, 1:2]
    theirs = ends[:, 1:2] + ends[:, 2:3] + ends[:, 3:4]
    a = jnp.where(bit, 1.0, jnp.exp(theirs))
    b = jnp.where(bit, jnp.exp(mine), 1.0)
    arrived = got[:, :body].astype(F32)
    packed = a * t[:, :body] + b * arrived
    diag = a * tails[:, :1] + b * ends[:, :1]
    level = mine + theirs
    if has_prefix:
        old = before[:, body:]
        e = jnp.where(bit, jnp.exp(old[:, 1:2]), 0.0)
        prefix = before[:, :body] + e * arrived
        prefix_diag = old[:, :1] + e * ends[:, :1]
        prefix_level = old[:, 1:2] + jnp.where(bit, theirs, 0.0)
    else:
        e = jnp.where(bit, jnp.ones_like(mine), 0.0)
        prefix = e * arrived
        prefix_diag = e * ends[:, :1]
        prefix_level = jnp.where(bit, theirs, 0.0)
    r = rows_of((8, width))
    sent[:, :body] = packed.astype(BF16)
    for h in range(half):
        sent[h, body:] = tail_sent(diag[h], level[h])
    before_new[:, :body] = prefix
    for h in range(half):
        before_new[h, body:] = tail_rows(prefix_diag[h], prefix_level[h])
        coef[h] = jnp.where(r == 0, a[h], jnp.where(r == 1, b[h], jnp.where(r == 2, e[h], 0.0)))
    if goes_on:
        t_new[:, :body] = packed
        for h in range(half):
            t_new[h, body:] = tail_rows(diag[h], level[h])


def join_state_kernel(has_prefix, goes_on, coef, t, got, *rest):
    sent, before_new = rest[has_prefix : has_prefix + 2]
    before = rest[0]
    t_new = rest[-1]
    for h in range(t.shape[0]):
        c = coef[h]
        arrived = got[h].astype(F32)
        new = c[0:1] * t[h] + c[1:2] * arrived
        if goes_on:
            t_new[h] = new
        sent[h] = new.astype(BF16)
        add = c[2:3] * arrived
        before_new[h] = before[h] + add if has_prefix else add


def prepare_kernel(ridge, ks, kt, qo, qr, fo, fr, go, gr, q_s, m_s, e_s, base):
    pairs, _, tokens, width = ks.shape
    half = pairs // 2
    core = bit_of(0)
    beta = gates(go, gr, core, half)
    level = running_sum(gates(fo, fr, core, half))
    level_t = level.T
    scale_t = jnp.exp(level_t)
    square = (tokens, tokens)
    lower = rows_of(square) >= lanes_of(square)
    eye = (rows_of((width, width)) == lanes_of((width, width))).astype(F32)
    for side, qref in enumerate((qo, qr)):
        for h in range(half):
            p = h + side * half
            turned = kt[p, 0].astype(F32) + kt[p, 1].astype(F32)
            cross = dot(wide(split(turned * beta[p : p + 1])), tall((ks[p, 0], ks[p, 1])))
            base[p] = cross + ridge_of(ridge, core, h, half) * eye
            column = level_t[:, p : p + 1]
            m_s[p] = jnp.where(lower, jnp.exp(jnp.minimum(column - level[p : p + 1], 0.0)) * beta[p : p + 1], 0.0)
            e_s[p] = jnp.broadcast_to(scale_t[:, p : p + 1], square)
            q_s[p] = unit_rows(columns(qref, core, h, half, width).astype(F32))


def inverse_kernel(which, base, fo, fr, gf, before, got, s_s, p_s, a_s):
    half, width, _ = gf.shape
    body = width // 2
    pairs = 2 * half
    core = bit_of(0)
    first = core == 0
    bit = bit_of(which) == 1
    forget = gates(fo, fr, core, half)
    decay = jnp.exp(jnp.sum(forget, axis=1, keepdims=True))
    eye = (rows_of((width, width)) == lanes_of((width, width))).astype(F32)
    for h in range(half):
        tail = before[h, body:]
        ends = got[h, body:].astype(F32)
        e = jnp.where(bit, jnp.exp(tail[1:2]), 0.0)
        start = unpack(before[h, :body] + e * got[h, :body].astype(F32), tail[:1] + e * ends[:1])
        for side, is_early in enumerate((first, jnp.logical_not(first))):
            p = h + side * half
            other = h + (1 - side) * half
            gram = jnp.where(is_early, start, decay[other : other + 1] * start + gf[h])
            s_s[p, 0], s_s[p, 1] = split(gram)
            system = gram + base[p]
            bound = jnp.max(jnp.sum(jnp.abs(system), axis=0, keepdims=True), axis=1, keepdims=True)
            a_s[p, 0], a_s[p, 1] = split(system)
            p_s[p] = eye / bound

    def refine(_, carry):
        left = [eye - dot(a_s[p, 0], p_s[p].astype(BF16)) for p in range(pairs)]
        for p in range(pairs):
            now = p_s[p]
            p_s[p] = now + dot(now.astype(BF16), left[p].astype(BF16))
        return carry

    lax.fori_loop(0, NEWTON - 1, refine, 0)
    for start in range(0, pairs, half):
        group = range(start, start + half)
        left = []
        for p in group:
            left.append(eye - dot(wide((a_s[p, 0], a_s[p, 1])), tall(split(p_s[p]))))
        for p, rest in zip(group, left):
            now = p_s[p]
            p_s[p] = now + dot(now.astype(BF16), rest.astype(BF16))


def correct_kernel(ridge, q_s, kt, m_s, e_s, ks, s_s, p_s, vo, vr, xs, part, x_s):
    pairs, _, width = q_s.shape
    half = pairs // 2
    core = bit_of(0)

    def both_of(p, i):
        return jnp.concatenate([s_s[p, i], kt[p, i]], axis=1)

    for p in range(pairs):
        x_s[p] = dot(q_s[p].astype(BF16), p_s[p].astype(BF16))

    def correct(_, carry):
        both = [dot(x_s[p].astype(BF16), both_of(p, 0)) for p in range(pairs)]
        applied = []
        for p in range(pairs):
            scores = m_s[p] * both[p][:, width:]
            applied.append(
                e_s[p] * both[p][:, :width]
                + dot(scores.astype(BF16), ks[p, 0])
                + ridge_of(ridge, core, p % half, half) * x_s[p]
            )
        for p in range(pairs):
            x_s[p] = x_s[p] + dot((q_s[p] - applied[p]).astype(BF16), p_s[p].astype(BF16))
        return carry

    lax.fori_loop(0, CORR - 2, correct, 0)

    for start, vref in ((0, vo), (half, vr)):
        group = range(start, start + half)
        both = [dot(wide(split(x_s[p])), tall((both_of(p, 0), both_of(p, 1)))) for p in group]
        applied = []
        for p, found in zip(group, both):
            scores = m_s[p] * found[:, width:]
            applied.append(
                e_s[p] * found[:, :width]
                + dot(scores.astype(BF16), ks[p, 0])
                + ridge_of(ridge, core, p - start, half) * x_s[p]
            )
        solved = []
        for p, found in zip(group, applied):
            x = x_s[p] + dot((q_s[p] - found).astype(BF16), p_s[p].astype(BF16))
            solved.append(split(x))
            xs[p, 0], xs[p, 1] = solved[-1]
        scores = []
        for p, x in zip(group, solved):
            scores.append(m_s[p] * dot(wide(x), tall((kt[p, 0], kt[p, 1]))))
        for p, found in zip(group, scores):
            v = columns(vref, core, p - start, half, width)
            sh, sl = split(found)
            part[p] = dot(jnp.concatenate([sh, sl], axis=1), jnp.concatenate([v, v], axis=0))


def read_kernel(which, xs, part, e_s, fo, fr, uf, before_g, before, got, gain, y_own, y_other):
    half = uf.shape[0]
    width = uf.shape[1]
    body = width // 2
    core = bit_of(0)
    first = core == 0
    bit = bit_of(which) == 1
    decay = jnp.exp(jnp.sum(gates(fo, fr, core, half), axis=1, keepdims=True))
    sides = ((y_own, first), (y_other, jnp.logical_not(first)))
    for h in range(half):
        cols = slice(h * width, (h + 1) * width)
        e = jnp.where(bit, jnp.exp(before_g[h, body + 1 : body + 2]), 0.0)
        start = before[h] + e * got[h].astype(F32)
        scale = columns(gain, core, h, half, width)
        for side, (out, is_early) in enumerate(sides):
            p = h + side * half
            other = h + (1 - side) * half
            state = jnp.where(is_early, start, decay[other : other + 1] * start + uf[h])
            read = dot(wide((xs[p, 0], xs[p, 1])), tall(split(state)))
            o = e_s[p] * read + part[p]
            o = o * lax.rsqrt(jnp.mean(o * o, axis=-1, keepdims=True) + 1e-6)
            out[:, cols] = (o * scale).astype(BF16)


def stack_kernel(a, b, out):
    out[: a.shape[0]] = a[...]
    out[a.shape[0] :] = b[...]


def gathered_rows(y_own, y_other, y):
    core = bit_of(0)
    size = y_own.shape[1]
    y[:, pl.ds(pl.multiple_of(core * size, size), size)] = y_own[...]
    y[:, pl.ds(pl.multiple_of((1 - core) * size, size), size)] = y_other[...]


def project_kernel(table, chips, shares, y_own, y_other, own, other, *rest):
    out, y = rest[-2:]
    core = bit_of(0)
    place = lax.axis_index("seq") >> 1
    share = lax.axis_index("parts")
    gathered_rows(y_own, y_other, y)
    width = 2 * own.shape[0]
    size = own.shape[1] // shares
    tokens = y.shape[0]
    lefts = []
    for offset in range(chips):
        chip = jnp.bitwise_xor(place, offset)
        rows = y[:, pl.ds(pl.multiple_of(chip * width, width), width)].astype(F32)
        rows = jnp.where(core == 0, rows, pltpu.roll(rows, width // 2, 1))
        lefts.append(rows.astype(BF16))
    for q in range(shares):
        where = pl.ds(pl.multiple_of(jnp.bitwise_xor(share, q) * size, size), size)
        total = jnp.zeros((tokens, size), F32)
        for offset in range(0, chips, 2):
            blocks = []
            for o in (offset, offset + 1):
                for flip in (0, 1):
                    if o == 0:
                        blocks.append((own, other)[flip][:, where])
                    elif (o, flip, None) in table:
                        blocks.append(rest[table[o, flip, None][0]][:, where])
                    else:
                        piece, i = table[o, flip, q]
                        blocks.append(rest[piece][i])
            left = jnp.concatenate([lefts[offset], lefts[offset + 1]], axis=1)
            total = total + dot(left, jnp.concatenate(blocks, axis=0))
        out[:, where] = total.astype(BF16)


def project_copy_kernel(table, y_own, y_other, own, other, *rest):
    pieces = rest[:-4]
    out, w, y, sem = rest[-4:]
    core = bit_of(0)
    place = lax.axis_index("seq") >> 1
    share = lax.axis_index("parts")
    rows = own.shape[0]
    size = pieces[0].shape[2]

    def at(offset, flip):
        row = (jnp.bitwise_xor(place, offset) * 2 + jnp.bitwise_xor(core, flip)) * rows
        return pl.ds(pl.multiple_of(row, rows), rows)

    copies = [
        pltpu.make_async_copy(own, w.at[at(0, 0)], sem.at[0]),
        pltpu.make_async_copy(other, w.at[at(0, 1)], sem.at[1]),
    ]
    for (offset, flip, q), (piece, i) in table.items():
        where = pl.ds(pl.multiple_of(jnp.bitwise_xor(share, q) * size, size), size)
        copies.append(
            pltpu.make_async_copy(pieces[piece].at[i], w.at[at(offset, flip), where], sem.at[len(copies)])
        )
    for copy in copies:
        copy.start()
    gathered_rows(y_own, y_other, y)
    for copy in copies:
        copy.wait()
    out[...] = dot(y[...], w[...]).astype(BF16)


SMEM = pltpu.SMEM


def call(kernel, outs, scalars, ins, scratch=(), far=()):
    spec = pl.BlockSpec(memory_space=VMEM)
    near = [pltpu.with_memory_space_constraint(a, VMEM) for a in ins]
    far = [pltpu.with_memory_space_constraint(a, pltpu.HBM) for a in far]
    return pl.pallas_call(
        kernel,
        out_shape=outs,
        in_specs=[pl.BlockSpec(memory_space=SMEM)] * len(scalars)
        + [spec] * len(near)
        + [pl.BlockSpec(memory_space=pltpu.HBM)] * len(far),
        out_specs=jax.tree.map(lambda _: spec, outs),
        scratch_shapes=scratch,
        compiler_params=pltpu.CompilerParams(vmem_limit_bytes=GRANT),
    )(*scalars, *near, *far)


def on_device(mesh, queries, keys, values, log_forget, input_gate, ridge, gain, out_weight):
    sections, parts = mesh.shape["seq"], mesh.shape["parts"]
    tokens, features = keys.shape
    heads = log_forget.shape[0]
    width = features // heads
    half = heads // 2
    pairs = 2 * half
    body = width // 2
    chips = sections // 2
    bits = chips.bit_length() - 1
    rows, out_columns = out_weight.shape

    def swap(array, distance, axis="seq"):
        count = mesh.shape[axis]
        return lax.ppermute(array, axis, [(i, i ^ distance) for i in range(count)])

    keys_o = swap(keys, 1)
    forget_o, gate_o = swap(log_forget, 1), swap(input_gate, 1)
    values_o, queries_o = swap(values, 1), swap(queries, 1)
    mine = VMEM((tokens, half * width), BF16)
    small = VMEM(log_forget.shape, F32)
    size = out_columns // parts
    far_args = (out_weight, keys, values, queries, log_forget, input_gate)
    far_args += (gain.reshape(1, features), ridge.reshape(1, heads))
    own, keys_m, values_m, queries_m, forget_m, gate_m, gain_row, ridge_row = call(
        load_kernel,
        (VMEM((1, rows, size), BF16), mine, mine, mine, small, small, VMEM((1, features), F32), VMEM((1, heads), F32)),
        (),
        (),
        (pltpu.SemaphoreType.DMA((len(far_args),)),),
        far_args,
    )
    forgets = (forget_m, forget_o)
    gate_args = (*forgets, gate_m, gate_o)

    packed = (half, body + 8, width)
    sent = (half, body + 16, width)
    full = (half, width, width)
    many = (pairs, width, width)
    two = (pairs, 2, width, width)

    pg, tg, pw, tw, gf, uf, ks, kt = call(
        sums_kernel,
        (VMEM(sent, BF16), VMEM(packed, F32), VMEM(full, BF16), VMEM(full, F32), VMEM(full, F32), VMEM(full, F32),
         VMEM(two, BF16), VMEM(two, BF16)),
        (),
        (keys_m, keys_o, values_m, values_o, *gate_args),
    )

    before = before_w = None
    tg, tw = (tg,), (tw,)
    for r in range(bits):
        got = swap(pg, 2 << r)
        got_w = swap(pw, 2 << r)
        if r == bits - 1:
            break
        extra = () if before is None else (before,)
        goes_on = r < bits - 2
        pg, before, coef, *tg = call(
            functools.partial(join_kernel, r + 1, len(extra), goes_on),
            (VMEM(sent, BF16), VMEM(packed, F32), VMEM((half, 8, width), F32), *[VMEM(packed, F32)] * goes_on),
            (),
            (*tg, got, *extra),
        )
        extra = () if before_w is None else (before_w,)
        pw, before_w, *tw = call(
            functools.partial(join_state_kernel, len(extra), goes_on),
            (VMEM(full, BF16), VMEM(full, F32), *[VMEM(full, F32)] * goes_on),
            (),
            (coef, *tw, got_w, *extra),
        )
    last = bits

    def stack(a, b):
        return call(stack_kernel, VMEM((a.shape[0] + b.shape[0], rows, size), BF16), (), (a, b))

    table, pieces = {}, []

    def keep(offsets, q, array, flip):
        for i, offset in enumerate(offsets):
            table[offset, flip, q] = (len(pieces), i)
        pieces.append(array)

    groups = []
    if bits == 3:
        far, mid = swap(own, 8), swap(own, 4)
        farther = swap(far, 4)
        near = swap(out_weight, 2)
        both = stack(far, mid)
        groups.append(((4, 2), both))
        groups.append(((6, 7), stack(farther, swap(farther, 2))))
        keep((1,), None, near, 0)
        keep((1,), None, swap(near, 1), 1)
    else:
        held = ((0,), own)
        for bit in reversed(range(bits)):
            fresh = (tuple(o ^ (1 << bit) for o in held[0]), swap(held[1], 2 << bit))
            groups.append(fresh)
            if bit:
                held = (held[0] + fresh[0], stack(held[1], fresh[1]))
    for g, (offsets, array) in enumerate(groups):
        shares = [(0, array)]
        step = 1
        while step < parts:
            shares += [(q ^ step, swap(a, step, "parts")) for q, a in shares]
            step *= 2
        if bits == 3 and g == 0:
            shares += [(q + parts, swap(a, 2)) for q, a in shares]
        for q, a in shares:
            at = offsets if q < parts else tuple(o ^ 1 for o in offsets)
            keep(at, q % parts, a, 0)
            keep(at, q % parts, swap(a, 1), 1)
    weight_o = swap(out_weight, 1)

    q_s, m_s, e_s, base = call(
        prepare_kernel,
        (VMEM(many, F32), VMEM(many, F32), VMEM(many, F32), VMEM(many, F32)),
        (),
        (ridge_row, ks, kt, queries_m, queries_o, *gate_args),
    )
    s_s, p_s = call(
        functools.partial(inverse_kernel, last),
        (VMEM(two, BF16), VMEM(many, F32)),
        (),
        (base, *forgets, gf, before, got),
        (VMEM(two, BF16),),
    )
    xs, part = call(
        correct_kernel,
        (VMEM(two, BF16), VMEM(many, F32)),
        (),
        (ridge_row, q_s, kt, m_s, e_s, ks, s_s, p_s, values_m, values_o),
        (VMEM(many, F32),),
    )
    y_own, y_other = call(
        functools.partial(read_kernel, last),
        (VMEM((tokens, half * width), BF16),) * 2,
        (),
        (xs, part, e_s, *forgets, uf, before, before_w, got_w, gain_row),
    )
    y_got = swap(y_other, 1)

    result = jax.ShapeDtypeStruct((tokens, out_columns), BF16)
    y_full = VMEM((tokens, features), BF16)
    if bits == 3 and 2 * rows == width:
        return call(
            functools.partial(project_kernel, table, chips, parts),
            result,
            (),
            (y_own, y_got, out_weight, weight_o, *pieces),
            (y_full,),
        )
    here = pl.BlockSpec(memory_space=VMEM)
    return pl.pallas_call(
        functools.partial(project_copy_kernel, table),
        out_shape=result,
        in_specs=[here, here] + [pl.BlockSpec(memory_space=pl.ANY)] * (2 + len(pieces)),
        out_specs=here,
        scratch_shapes=[
            VMEM((features, out_columns), BF16), y_full, pltpu.SemaphoreType.DMA((2 + len(table),))
        ],
    )(y_own, y_got, out_weight, weight_o, *pieces)


def solution(mesh):
    rows = P(("parts", "seq"), None)
    gate = P(None, ("parts", "seq"))

    def body(*args):
        return on_device(mesh, *args)

    return jax.shard_map(
        body,
        mesh=mesh,
        in_specs=(rows, rows, rows, gate, gate, P(), P(), P("seq", None)),
        out_specs=rows,
        check_vma=False,
    )
```

```python
import functools
import jax
import jax.numpy as jnp
from jax import lax
from jax.experimental import pallas as pl
from jax.experimental.pallas import tpu as pltpu
from jax.sharding import PartitionSpec as P

NEWTON = 6
CORR = 4
F32 = jnp.float32
BF16 = jnp.bfloat16
EXACT = lax.Precision.HIGHEST
VMEM = pltpu.VMEM
STRIPS = 2
GRANT = 8 * 1024 * 1024


def rows_of(shape):
    return lax.broadcasted_iota(jnp.int32, shape, 0)


def lanes_of(shape):
    return lax.broadcasted_iota(jnp.int32, shape, 1)


def bit_of(i):
    return (lax.axis_index("seq") >> i) & 1


def split(x):
    high = x.astype(BF16)
    return high, (x - high.astype(F32)).astype(BF16)


def dot(a, b):
    return jnp.dot(a, b, preferred_element_type=F32)


def wide(pair):
    high, low = pair
    return jnp.concatenate([high, low, high], axis=1)


def beside(pair):
    return jnp.concatenate(pair, axis=1)


def twice(right):
    return jnp.concatenate([right, right], axis=0)


def tall(pair):
    high, low = pair
    return jnp.concatenate([high, high, low], axis=0)


def unit_rows(x):
    return x * lax.rsqrt(jnp.sum(x * x, axis=-1, keepdims=True) + 1e-6)


def pick(first, own, other):
    return jnp.where(first, own, other)


def columns(ref, core, h, half, width):
    if ref.shape[1] == half * width:
        return ref[:, h * width : (h + 1) * width]
    return ref[:, pl.ds(pl.multiple_of((core * half + h) * width, width), width)]


def gates(own_ref, other_ref, core, half):
    own, other = own_ref[...], other_ref[...]
    return jnp.concatenate(
        [
            jnp.where(core == 0, own[:half], own[half:]),
            jnp.where(core == 0, other[:half], other[half:]),
        ],
        axis=0,
    )


def ridge_of(row, core, h, half):
    return jnp.where(core == 0, row[:, h : h + 1], row[:, half + h : half + h + 1])


def running_sum(a):
    width = a.shape[-1]
    tri = (rows_of((width, width)) <= lanes_of((width, width))).astype(F32)
    return jnp.dot(a, tri, precision=EXACT, preferred_element_type=F32)


def pack(sym):
    width = sym.shape[0]
    half = width // 2
    top, low = sym[:half], pltpu.roll(sym[half:], half, 1)
    shape = (half, width)
    r, c = rows_of(shape), lanes_of(shape)
    body = jnp.where(r > c, low, top)
    diag = jnp.sum(jnp.where(r == c, low, 0.0), axis=0, keepdims=True)
    return body, diag


def unpack(body, diag):
    half, _ = body.shape
    r, c = rows_of(body.shape), lanes_of(body.shape)
    top = jnp.where(c > r, body, 0.0) + jnp.where(c == r, 0.5 * body, 0.0)
    low = jnp.where(c < r, body, 0.0) + jnp.where(c == r, 0.5 * diag, 0.0)
    full = jnp.concatenate([top, pltpu.roll(low, half, 1)], axis=0)
    return full + full.T


def tail_rows(diag, level):
    r = rows_of((8, diag.shape[-1]))
    return jnp.where(r == 0, diag, jnp.where(r == 1, level, 0.0))


def tail_sent(diag, level):
    one = level.astype(BF16).astype(F32)
    two = (level - one).astype(BF16).astype(F32)
    three = level - one - two
    r = rows_of((16, diag.shape[-1]))
    out = jnp.where(r == 0, diag, jnp.where(r == 1, one, jnp.where(r == 2, two, jnp.where(r == 3, three, 0.0))))
    return out.astype(BF16)


def load_kernel(*refs):
    count = (len(refs) - 1) // 2
    sources, outs, sem = refs[:count], refs[count : 2 * count], refs[-1]
    copies = []
    for i, (source, out) in enumerate(zip(sources, outs)):
        if len(out.shape) == 3:
            size = out.shape[2]
            share = lax.axis_index("parts")
            source, out = source.at[:, pl.ds(pl.multiple_of(share * size, size), size)], out.at[0]
        elif out.shape[1] < source.shape[1]:
            size = out.shape[1]
            source = source.at[:, pl.ds(pl.multiple_of(bit_of(0) * size, size), size)]
        copies.append(pltpu.make_async_copy(source, out, sem.at[i]))
    for copy in copies:
        copy.start()
    for copy in copies:
        copy.wait()


def sums_kernel(ko, kr, vo, vr, fo, fr, go, gr, pg, tg, pw, tw, gf, uf, ks, kt):
    half = gf.shape[0]
    width = gf.shape[1]
    body = width // 2
    core = bit_of(0)
    forget = gates(fo, fr, core, half)
    beta = gates(go, gr, core, half)
    level = running_sum(forget)
    last = level[:, width - 1 :]
    tails = jnp.exp(last - level) * beta
    decay = jnp.exp(last)
    first = core == 0
    weighted = {}
    for h in range(half):
        grams = []
        for side, kref in enumerate((ko, kr)):
            p = h + side * half
            k = unit_rows(columns(kref, core, h, half, width).astype(F32))
            turned = k.T
            kk = split(k)
            ks[p, 0], ks[p, 1] = kk
            kt[p, 0], kt[p, 1] = split(turned)
            weighted[p] = split(turned * tails[p : p + 1])
            grams.append(dot(beside(weighted[p]), twice(kk[0])))
        early = pick(first, grams[0], grams[1])
        late = pick(first, grams[1], grams[0])
        shrink = pick(first, decay[half + h : half + h + 1], decay[h : h + 1])
        gf[h] = early
        packed, diag = pack(shrink * early + late)
        total = jnp.broadcast_to(last[h : h + 1] + last[half + h : half + h + 1], (1, width))
        tg[h, :body] = packed
        tg[h, body:] = tail_rows(diag, total)
        pg[h, :body] = packed.astype(BF16)
        pg[h, body:] = tail_sent(diag, total)
    for h in range(half):
        states = []
        for side, vref in enumerate((vo, vr)):
            v = columns(vref, core, h, half, width)
            states.append(
                dot(beside(weighted[h + side * half]), twice(v))
            )
        early_state = pick(first, states[0], states[1])
        late_state = pick(first, states[1], states[0])
        shrink = pick(first, decay[half + h : half + h + 1], decay[h : h + 1])
        uf[h] = early_state
        state = shrink * early_state + late_state
        tw[h] = state
        pw[h] = state.astype(BF16)


def join_kernel(which, has_prefix, goes_on, t, got, *rest):
    sent, before_new, coef = rest[has_prefix : has_prefix + 3]
    before = rest[0]
    t_new = rest[-1]
    bit = bit_of(which) == 1
    half, rows, width = t.shape
    body = rows - 8
    tails = t[:, body:]
    ends = got[:, body:].astype(F32)
    mine = tails[:, 1:2]
    theirs = ends[:, 1:2] + ends[:, 2:3] + ends[:, 3:4]
    a = jnp.where(bit, 1.0, jnp.exp(theirs))
    b = jnp.where(bit, jnp.exp(mine), 1.0)
    arrived = got[:, :body].astype(F32)
    packed = a * t[:, :body] + b * arrived
    diag = a * tails[:, :1] + b * ends[:, :1]
    level = mine + theirs
    if has_prefix:
        old = before[:, body:]
        e = jnp.where(bit, jnp.exp(old[:, 1:2]), 0.0)
        prefix = before[:, :body] + e * arrived
        prefix_diag = old[:, :1] + e * ends[:, :1]
        prefix_level = old[:, 1:2] + jnp.where(bit, theirs, 0.0)
    else:
        e = jnp.where(bit, jnp.ones_like(mine), 0.0)
        prefix = e * arrived
        prefix_diag = e * ends[:, :1]
        prefix_level = jnp.where(bit, theirs, 0.0)
    r = rows_of((8, width))
    sent[:, :body] = packed.astype(BF16)
    for h in range(half):
        sent[h, body:] = tail_sent(diag[h], level[h])
    before_new[:, :body] = prefix
    for h in range(half):
        before_new[h, body:] = tail_rows(prefix_diag[h], prefix_level[h])
        coef[h] = jnp.where(r == 0, a[h], jnp.where(r == 1, b[h], jnp.where(r == 2, e[h], 0.0)))
    if goes_on:
        t_new[:, :body] = packed
        for h in range(half):
            t_new[h, body:] = tail_rows(diag[h], level[h])


def join_state_kernel(has_prefix, goes_on, coef, t, got, *rest):
    sent, before_new = rest[has_prefix : has_prefix + 2]
    before = rest[0]
    t_new = rest[-1]
    for h in range(t.shape[0]):
        c = coef[h]
        arrived = got[h].astype(F32)
        new = c[0:1] * t[h] + c[1:2] * arrived
        if goes_on:
            t_new[h] = new
        sent[h] = new.astype(BF16)
        add = c[2:3] * arrived
        before_new[h] = before[h] + add if has_prefix else add


def prepare_kernel(ridge, ks, kt, qo, qr, fo, fr, go, gr, q_s, m_s, e_s, base):
    pairs, _, tokens, width = ks.shape
    half = pairs // 2
    core = bit_of(0)
    beta = gates(go, gr, core, half)
    level = running_sum(gates(fo, fr, core, half))
    level_t = level.T
    scale_t = jnp.exp(level_t)
    square = (tokens, tokens)
    lower = rows_of(square) >= lanes_of(square)
    eye = (rows_of((width, width)) == lanes_of((width, width))).astype(F32)
    for side, qref in enumerate((qo, qr)):
        for h in range(half):
            p = h + side * half
            turned = kt[p, 0].astype(F32) + kt[p, 1].astype(F32)
            cross = dot(beside(split(turned * beta[p : p + 1])), twice(ks[p, 0]))
            base[p] = cross + ridge_of(ridge, core, h, half) * eye
            column = level_t[:, p : p + 1]
            m_s[p] = jnp.where(lower, jnp.exp(jnp.minimum(column - level[p : p + 1], 0.0)) * beta[p : p + 1], 0.0)
            e_s[p] = jnp.broadcast_to(scale_t[:, p : p + 1], square)
            q_s[p] = unit_rows(columns(qref, core, h, half, width).astype(F32))


def inverse_kernel(which, base, fo, fr, gf, before, got, s_s, p_s, a_s):
    half, width, _ = gf.shape
    body = width // 2
    pairs = 2 * half
    core = bit_of(0)
    first = core == 0
    bit = bit_of(which) == 1
    forget = gates(fo, fr, core, half)
    decay = jnp.exp(jnp.sum(forget, axis=1, keepdims=True))
    eye = (rows_of((width, width)) == lanes_of((width, width))).astype(F32)
    for h in range(half):
        tail = before[h, body:]
        ends = got[h, body:].astype(F32)
        e = jnp.where(bit, jnp.exp(tail[1:2]), 0.0)
        start = unpack(before[h, :body] + e * got[h, :body].astype(F32), tail[:1] + e * ends[:1])
        for side, is_early in enumerate((first, jnp.logical_not(first))):
            p = h + side * half
            other = h + (1 - side) * half
            gram = jnp.where(is_early, start, decay[other : other + 1] * start + gf[h])
            s_s[p, 0], s_s[p, 1] = split(gram)
            system = gram + base[p]
            bound = jnp.max(jnp.sum(jnp.abs(system), axis=0, keepdims=True), axis=1, keepdims=True)
            a_s[p] = system.astype(BF16)
            p_s[p] = eye / bound

    def refine(_, carry):
        left = [eye - dot(a_s[p], p_s[p].astype(BF16)) for p in range(pairs)]
        for p in range(pairs):
            now = p_s[p]
            p_s[p] = now + dot(now.astype(BF16), left[p].astype(BF16))
        return carry

    lax.fori_loop(0, NEWTON - 1, refine, 0)
    for start in range(0, pairs, half):
        group = range(start, start + half)
        left = []
        for p in group:
            high = a_s[p]
            left.append(eye - dot(beside((high, high)), jnp.concatenate(split(p_s[p]), axis=0)))
        for p, rest in zip(group, left):
            now = p_s[p]
            p_s[p] = now + dot(now.astype(BF16), rest.astype(BF16))


def correct_kernel(ridge, q_s, kt, m_s, e_s, ks, s_s, p_s, vo, vr, xs, part, x_s):
    pairs, _, width = q_s.shape
    half = pairs // 2
    core = bit_of(0)

    def both_of(p, i):
        return jnp.concatenate([s_s[p, i], kt[p, i]], axis=1)

    for p in range(pairs):
        x_s[p] = dot(q_s[p].astype(BF16), p_s[p].astype(BF16))

    def correct(_, carry):
        both = [dot(x_s[p].astype(BF16), both_of(p, 0)) for p in range(pairs)]
        applied = []
        for p in range(pairs):
            scores = m_s[p] * both[p][:, width:]
            applied.append(
                e_s[p] * both[p][:, :width]
                + dot(scores.astype(BF16), ks[p, 0])
                + ridge_of(ridge, core, p % half, half) * x_s[p]
            )
        for p in range(pairs):
            x_s[p] = x_s[p] + dot((q_s[p] - applied[p]).astype(BF16), p_s[p].astype(BF16))
        return carry

    lax.fori_loop(0, CORR - 2, correct, 0)

    for start, vref in ((0, vo), (half, vr)):
        group = range(start, start + half)
        both = [dot(wide(split(x_s[p])), tall((both_of(p, 0), both_of(p, 1)))) for p in group]
        applied = []
        for p, found in zip(group, both):
            scores = m_s[p] * found[:, width:]
            applied.append(
                e_s[p] * found[:, :width]
                + dot(scores.astype(BF16), ks[p, 0])
                + ridge_of(ridge, core, p - start, half) * x_s[p]
            )
        solved = []
        for p, found in zip(group, applied):
            x = x_s[p] + dot((q_s[p] - found).astype(BF16), p_s[p].astype(BF16))
            solved.append(split(x))
            xs[p, 0], xs[p, 1] = solved[-1]
        scores = []
        for p, x in zip(group, solved):
            scores.append(m_s[p] * dot(wide(x), tall((kt[p, 0], kt[p, 1]))))
        for p, found in zip(group, scores):
            v = columns(vref, core, p - start, half, width)
            sh, sl = split(found)
            part[p] = dot(beside((sh, sl)), twice(v))


def read_kernel(which, xs, part, e_s, fo, fr, uf, before_g, before, got, gain, y_own, y_other):
    half = uf.shape[0]
    width = uf.shape[1]
    body = width // 2
    core = bit_of(0)
    first = core == 0
    bit = bit_of(which) == 1
    decay = jnp.exp(jnp.sum(gates(fo, fr, core, half), axis=1, keepdims=True))
    sides = ((y_own, first), (y_other, jnp.logical_not(first)))
    for h in range(half):
        cols = slice(h * width, (h + 1) * width)
        e = jnp.where(bit, jnp.exp(before_g[h, body + 1 : body + 2]), 0.0)
        start = before[h] + e * got[h].astype(F32)
        scale = columns(gain, core, h, half, width)
        for side, (out, is_early) in enumerate(sides):
            p = h + side * half
            other = h + (1 - side) * half
            state = jnp.where(is_early, start, decay[other : other + 1] * start + uf[h])
            read = dot(wide((xs[p, 0], xs[p, 1])), tall(split(state)))
            o = e_s[p] * read + part[p]
            o = o * lax.rsqrt(jnp.mean(o * o, axis=-1, keepdims=True) + 1e-6)
            out[:, cols] = (o * scale).astype(BF16)


def stack_kernel(a, b, out):
    out[: a.shape[0]] = a[...]
    out[a.shape[0] :] = b[...]


def gathered_rows(y_own, y_other, y):
    core = bit_of(0)
    size = y_own.shape[1]
    y[:, pl.ds(pl.multiple_of(core * size, size), size)] = y_own[...]
    y[:, pl.ds(pl.multiple_of((1 - core) * size, size), size)] = y_other[...]


def project_kernel(table, chips, shares, y_own, y_other, own, other, *rest):
    result, y, out, sem = rest[-4:]
    core = bit_of(0)
    place = lax.axis_index("seq") >> 1
    share = lax.axis_index("parts")
    gathered_rows(y_own, y_other, y)
    width = 2 * own.shape[0]
    size = own.shape[1] // shares
    tokens = y.shape[0]
    lefts = []
    for offset in range(chips):
        chip = jnp.bitwise_xor(place, offset)
        rows = y[:, pl.ds(pl.multiple_of(chip * width, width), width)].astype(F32)
        rows = jnp.where(core == 0, rows, pltpu.roll(rows, width // 2, 1))
        lefts.append(rows.astype(BF16))
    copies = []
    strip = size // STRIPS
    for q in range(shares):
        for n in range(STRIPS):
            start = jnp.bitwise_xor(share, q) * size + n * strip
            where = pl.ds(pl.multiple_of(start, strip), strip)
            inner = slice(n * strip, (n + 1) * strip)
            total = jnp.zeros((tokens, strip), F32)
            for offset in range(0, chips, 2):
                blocks = []
                for o in (offset, offset + 1):
                    for flip in (0, 1):
                        if o == 0:
                            blocks.append((own, other)[flip][:, where])
                        elif (o, flip, None) in table:
                            blocks.append(rest[table[o, flip, None][0]][:, where])
                        else:
                            piece, i = table[o, flip, q]
                            blocks.append(rest[piece][i, :, inner])
                left = jnp.concatenate([lefts[offset], lefts[offset + 1]], axis=1)
                total = total + dot(left, jnp.concatenate(blocks, axis=0))
            out[:, where] = total.astype(BF16)
            copies.append(pltpu.make_async_copy(out.at[:, where], result.at[:, where], sem.at[len(copies)]))
            copies[-1].start()
    for copy in copies:
        copy.wait()


def project_copy_kernel(table, y_own, y_other, own, other, *rest):
    pieces = rest[:-4]
    out, w, y, sem = rest[-4:]
    core = bit_of(0)
    place = lax.axis_index("seq") >> 1
    share = lax.axis_index("parts")
    rows = own.shape[0]
    size = pieces[0].shape[2]

    def at(offset, flip):
        row = (jnp.bitwise_xor(place, offset) * 2 + jnp.bitwise_xor(core, flip)) * rows
        return pl.ds(pl.multiple_of(row, rows), rows)

    copies = [
        pltpu.make_async_copy(own, w.at[at(0, 0)], sem.at[0]),
        pltpu.make_async_copy(other, w.at[at(0, 1)], sem.at[1]),
    ]
    for (offset, flip, q), (piece, i) in table.items():
        where = pl.ds(pl.multiple_of(jnp.bitwise_xor(share, q) * size, size), size)
        copies.append(
            pltpu.make_async_copy(pieces[piece].at[i], w.at[at(offset, flip), where], sem.at[len(copies)])
        )
    for copy in copies:
        copy.start()
    gathered_rows(y_own, y_other, y)
    for copy in copies:
        copy.wait()
    out[...] = dot(y[...], w[...]).astype(BF16)


SMEM = pltpu.SMEM


def call(kernel, outs, scalars, ins, scratch=(), far=(), out_space=VMEM):
    spec = pl.BlockSpec(memory_space=VMEM)
    near = [pltpu.with_memory_space_constraint(a, VMEM) for a in ins]
    far = [pltpu.with_memory_space_constraint(a, pltpu.HBM) for a in far]
    return pl.pallas_call(
        kernel,
        out_shape=outs,
        in_specs=[pl.BlockSpec(memory_space=SMEM)] * len(scalars)
        + [spec] * len(near)
        + [pl.BlockSpec(memory_space=pltpu.HBM)] * len(far),
        out_specs=jax.tree.map(lambda _: pl.BlockSpec(memory_space=out_space), outs),
        scratch_shapes=scratch,
        compiler_params=pltpu.CompilerParams(vmem_limit_bytes=GRANT),
    )(*scalars, *near, *far)


def on_device(mesh, queries, keys, values, log_forget, input_gate, ridge, gain, out_weight):
    sections, parts = mesh.shape["seq"], mesh.shape["parts"]
    tokens, features = keys.shape
    heads = log_forget.shape[0]
    width = features // heads
    half = heads // 2
    pairs = 2 * half
    body = width // 2
    chips = sections // 2
    bits = chips.bit_length() - 1
    rows, out_columns = out_weight.shape

    def swap(array, distance, axis="seq"):
        count = mesh.shape[axis]
        return lax.ppermute(array, axis, [(i, i ^ distance) for i in range(count)])

    keys_o = swap(keys, 1)
    forget_o, gate_o = swap(log_forget, 1), swap(input_gate, 1)
    values_o, queries_o = swap(values, 1), swap(queries, 1)
    mine = VMEM((tokens, half * width), BF16)
    small = VMEM(log_forget.shape, F32)
    size = out_columns // parts
    far_args = (out_weight, keys, values, queries, log_forget, input_gate)
    far_args += (gain.reshape(1, features), ridge.reshape(1, heads))
    own, keys_m, values_m, queries_m, forget_m, gate_m, gain_row, ridge_row = call(
        load_kernel,
        (VMEM((1, rows, size), BF16), mine, mine, mine, small, small, VMEM((1, features), F32), VMEM((1, heads), F32)),
        (),
        (),
        (pltpu.SemaphoreType.DMA((len(far_args),)),),
        far_args,
    )
    forgets = (forget_m, forget_o)
    gate_args = (*forgets, gate_m, gate_o)

    packed = (half, body + 8, width)
    sent = (half, body + 16, width)
    full = (half, width, width)
    many = (pairs, width, width)
    two = (pairs, 2, width, width)

    pg, tg, pw, tw, gf, uf, ks, kt = call(
        sums_kernel,
        (VMEM(sent, BF16), VMEM(packed, F32), VMEM(full, BF16), VMEM(full, F32), VMEM(full, F32), VMEM(full, F32),
         VMEM(two, BF16), VMEM(two, BF16)),
        (),
        (keys_m, keys_o, values_m, values_o, *gate_args),
    )

    before = before_w = None
    tg, tw = (tg,), (tw,)
    for r in range(bits):
        got = swap(pg, 2 << r)
        got_w = swap(pw, 2 << r)
        if r == bits - 1:
            break
        extra = () if before is None else (before,)
        goes_on = r < bits - 2
        pg, before, coef, *tg = call(
            functools.partial(join_kernel, r + 1, len(extra), goes_on),
            (VMEM(sent, BF16), VMEM(packed, F32), VMEM((half, 8, width), F32), *[VMEM(packed, F32)] * goes_on),
            (),
            (*tg, got, *extra),
        )
        extra = () if before_w is None else (before_w,)
        pw, before_w, *tw = call(
            functools.partial(join_state_kernel, len(extra), goes_on),
            (VMEM(full, BF16), VMEM(full, F32), *[VMEM(full, F32)] * goes_on),
            (),
            (coef, *tw, got_w, *extra),
        )
    last = bits

    def stack(a, b):
        return call(stack_kernel, VMEM((a.shape[0] + b.shape[0], rows, size), BF16), (), (a, b))

    table, pieces = {}, []

    def keep(offsets, q, array, flip):
        for i, offset in enumerate(offsets):
            table[offset, flip, q] = (len(pieces), i)
        pieces.append(array)

    groups = []
    if bits == 3:
        far, mid = swap(own, 8), swap(own, 4)
        farther = swap(far, 4)
        near = swap(out_weight, 2)
        both = stack(far, mid)
        groups.append(((4, 2), both))
        groups.append(((6, 7), stack(farther, swap(farther, 2))))
        keep((1,), None, near, 0)
        keep((1,), None, swap(near, 1), 1)
    else:
        held = ((0,), own)
        for bit in reversed(range(bits)):
            fresh = (tuple(o ^ (1 << bit) for o in held[0]), swap(held[1], 2 << bit))
            groups.append(fresh)
            if bit:
                held = (held[0] + fresh[0], stack(held[1], fresh[1]))
    for g, (offsets, array) in enumerate(groups):
        shares = [(0, array)]
        step = 1
        while step < parts:
            shares += [(q ^ step, swap(a, step, "parts")) for q, a in shares]
            step *= 2
        if bits == 3 and g == 0:
            shares += [(q + parts, swap(a, 2)) for q, a in shares]
        for q, a in shares:
            at = offsets if q < parts else tuple(o ^ 1 for o in offsets)
            keep(at, q % parts, a, 0)
            keep(at, q % parts, swap(a, 1), 1)
    weight_o = swap(out_weight, 1)

    q_s, m_s, e_s, base = call(
        prepare_kernel,
        (VMEM(many, F32), VMEM(many, F32), VMEM(many, F32), VMEM(many, F32)),
        (),
        (ridge_row, ks, kt, queries_m, queries_o, *gate_args),
    )
    s_s, p_s = call(
        functools.partial(inverse_kernel, last),
        (VMEM(two, BF16), VMEM(many, F32)),
        (),
        (base, *forgets, gf, before, got),
        (VMEM(many, BF16),),
    )
    xs, part = call(
        correct_kernel,
        (VMEM(two, BF16), VMEM(many, F32)),
        (),
        (ridge_row, q_s, kt, m_s, e_s, ks, s_s, p_s, values_m, values_o),
        (VMEM(many, F32),),
    )
    y_own, y_other = call(
        functools.partial(read_kernel, last),
        (VMEM((tokens, half * width), BF16),) * 2,
        (),
        (xs, part, e_s, *forgets, uf, before, before_w, got_w, gain_row),
    )
    y_got = swap(y_other, 1)

    result = jax.ShapeDtypeStruct((tokens, out_columns), BF16)
    y_full = VMEM((tokens, features), BF16)
    if bits == 3 and 2 * rows == width:
        return call(
            functools.partial(project_kernel, table, chips, parts),
            result,
            (),
            (y_own, y_got, out_weight, weight_o, *pieces),
            (y_full, VMEM((tokens, out_columns), BF16), pltpu.SemaphoreType.DMA((parts * STRIPS,))),
            out_space=pl.ANY,
        )
    here = pl.BlockSpec(memory_space=VMEM)
    return pl.pallas_call(
        functools.partial(project_copy_kernel, table),
        out_shape=result,
        in_specs=[here, here] + [pl.BlockSpec(memory_space=pl.ANY)] * (2 + len(pieces)),
        out_specs=here,
        scratch_shapes=[
            VMEM((features, out_columns), BF16), y_full, pltpu.SemaphoreType.DMA((2 + len(table),))
        ],
    )(y_own, y_got, out_weight, weight_o, *pieces)


def solution(mesh):
    rows = P(("parts", "seq"), None)
    gate = P(None, ("parts", "seq"))

    def body(*args):
        return on_device(mesh, *args)

    return jax.shard_map(
        body,
        mesh=mesh,
        in_specs=(rows, rows, rows, gate, gate, P(), P(), P("seq", None)),
        out_specs=rows,
        check_vma=False,
    )
```

```python
import functools
import jax
import jax.numpy as jnp
from jax import lax
from jax.experimental import pallas as pl
from jax.experimental.pallas import tpu as pltpu
from jax.sharding import PartitionSpec as P

NEWTON = 6
CORR = 4
F32 = jnp.float32
BF16 = jnp.bfloat16
EXACT = lax.Precision.HIGHEST
VMEM = pltpu.VMEM
STRIPS = 2
GRANT = 8 * 1024 * 1024


def rows_of(shape):
    return lax.broadcasted_iota(jnp.int32, shape, 0)


def lanes_of(shape):
    return lax.broadcasted_iota(jnp.int32, shape, 1)


def bit_of(i):
    return (lax.axis_index("seq") >> i) & 1


def split(x):
    high = x.astype(BF16)
    return high, (x - high.astype(F32)).astype(BF16)


def dot(a, b):
    return jnp.dot(a, b, preferred_element_type=F32)


def wide(pair):
    high, low = pair
    return jnp.concatenate([high, low, high], axis=1)


def beside(pair):
    return jnp.concatenate(pair, axis=1)


def twice(right):
    return jnp.concatenate([right, right], axis=0)


def tall(pair):
    high, low = pair
    return jnp.concatenate([high, high, low], axis=0)


def unit_rows(x):
    return x * lax.rsqrt(jnp.sum(x * x, axis=-1, keepdims=True) + 1e-6)


def pick(first, own, other):
    return jnp.where(first, own, other)


def columns(ref, core, h, half, width):
    if ref.shape[1] == half * width:
        return ref[:, h * width : (h + 1) * width]
    return ref[:, pl.ds(pl.multiple_of((core * half + h) * width, width), width)]


def gates(own_ref, other_ref, core, half):
    own, other = own_ref[...], other_ref[...]
    return jnp.concatenate(
        [
            jnp.where(core == 0, own[:half], own[half:]),
            jnp.where(core == 0, other[:half], other[half:]),
        ],
        axis=0,
    )


def ridge_of(row, core, h, half):
    return jnp.where(core == 0, row[:, h : h + 1], row[:, half + h : half + h + 1])


def running_sum(a):
    width = a.shape[-1]
    tri = (rows_of((width, width)) <= lanes_of((width, width))).astype(F32)
    return jnp.dot(a, tri, precision=EXACT, preferred_element_type=F32)


def pack(sym):
    width = sym.shape[0]
    half = width // 2
    top, low = sym[:half], pltpu.roll(sym[half:], half, 1)
    shape = (half, width)
    r, c = rows_of(shape), lanes_of(shape)
    body = jnp.where(r > c, low, top)
    diag = jnp.sum(jnp.where(r == c, low, 0.0), axis=0, keepdims=True)
    return body, diag


def unpack(body, diag):
    half, _ = body.shape
    r, c = rows_of(body.shape), lanes_of(body.shape)
    top = jnp.where(c > r, body, 0.0) + jnp.where(c == r, 0.5 * body, 0.0)
    low = jnp.where(c < r, body, 0.0) + jnp.where(c == r, 0.5 * diag, 0.0)
    full = jnp.concatenate([top, pltpu.roll(low, half, 1)], axis=0)
    return full + full.T


def tail_rows(diag, level):
    r = rows_of((8, diag.shape[-1]))
    return jnp.where(r == 0, diag, jnp.where(r == 1, level, 0.0))


def tail_sent(diag, level):
    one = level.astype(BF16).astype(F32)
    two = (level - one).astype(BF16).astype(F32)
    three = level - one - two
    r = rows_of((16, diag.shape[-1]))
    out = jnp.where(r == 0, diag, jnp.where(r == 1, one, jnp.where(r == 2, two, jnp.where(r == 3, three, 0.0))))
    return out.astype(BF16)


def load_kernel(*refs):
    count = (len(refs) - 1) // 2
    sources, outs, sem = refs[:count], refs[count : 2 * count], refs[-1]
    copies = []
    for i, (source, out) in enumerate(zip(sources, outs)):
        if len(out.shape) == 3:
            size = out.shape[2]
            share = lax.axis_index("parts")
            source, out = source.at[:, pl.ds(pl.multiple_of(share * size, size), size)], out.at[0]
        elif out.shape[1] < source.shape[1]:
            size = out.shape[1]
            source = source.at[:, pl.ds(pl.multiple_of(bit_of(0) * size, size), size)]
        copies.append(pltpu.make_async_copy(source, out, sem.at[i]))
    for copy in copies:
        copy.start()
    for copy in copies:
        copy.wait()


def sums_kernel(ko, kr, vo, vr, fo, fr, go, gr, pg, tg, pw, tw, gf, uf, ks, kt):
    half = gf.shape[0]
    width = gf.shape[1]
    body = width // 2
    core = bit_of(0)
    forget = gates(fo, fr, core, half)
    beta = gates(go, gr, core, half)
    level = running_sum(forget)
    last = level[:, width - 1 :]
    tails = jnp.exp(last - level) * beta
    decay = jnp.exp(last)
    first = core == 0
    weighted = {}
    for h in range(half):
        grams = []
        for side, kref in enumerate((ko, kr)):
            p = h + side * half
            k = unit_rows(columns(kref, core, h, half, width).astype(F32))
            turned = k.T
            kk = split(k)
            ks[p, 0], ks[p, 1] = kk
            kt[p, 0], kt[p, 1] = split(turned)
            weighted[p] = split(turned * tails[p : p + 1])
            grams.append(dot(beside(weighted[p]), twice(kk[0])))
        early = pick(first, grams[0], grams[1])
        late = pick(first, grams[1], grams[0])
        shrink = pick(first, decay[half + h : half + h + 1], decay[h : h + 1])
        gf[h] = early
        packed, diag = pack(shrink * early + late)
        total = jnp.broadcast_to(last[h : h + 1] + last[half + h : half + h + 1], (1, width))
        tg[h, :body] = packed
        tg[h, body:] = tail_rows(diag, total)
        pg[h, :body] = packed.astype(BF16)
        pg[h, body:] = tail_sent(diag, total)
    for h in range(half):
        states = []
        for side, vref in enumerate((vo, vr)):
            v = columns(vref, core, h, half, width)
            states.append(
                dot(beside(weighted[h + side * half]), twice(v))
            )
        early_state = pick(first, states[0], states[1])
        late_state = pick(first, states[1], states[0])
        shrink = pick(first, decay[half + h : half + h + 1], decay[h : h + 1])
        uf[h] = early_state
        state = shrink * early_state + late_state
        tw[h] = state
        pw[h] = state.astype(BF16)


def join_kernel(which, has_prefix, goes_on, t, got, *rest):
    sent, before_new, coef = rest[has_prefix : has_prefix + 3]
    before = rest[0]
    t_new = rest[-1]
    bit = bit_of(which) == 1
    half, rows, width = t.shape
    body = rows - 8
    tails = t[:, body:]
    ends = got[:, body:].astype(F32)
    mine = tails[:, 1:2]
    theirs = ends[:, 1:2] + ends[:, 2:3] + ends[:, 3:4]
    a = jnp.where(bit, 1.0, jnp.exp(theirs))
    b = jnp.where(bit, jnp.exp(mine), 1.0)
    arrived = got[:, :body].astype(F32)
    packed = a * t[:, :body] + b * arrived
    diag = a * tails[:, :1] + b * ends[:, :1]
    level = mine + theirs
    if has_prefix:
        old = before[:, body:]
        e = jnp.where(bit, jnp.exp(old[:, 1:2]), 0.0)
        prefix = before[:, :body] + e * arrived
        prefix_diag = old[:, :1] + e * ends[:, :1]
        prefix_level = old[:, 1:2] + jnp.where(bit, theirs, 0.0)
    else:
        e = jnp.where(bit, jnp.ones_like(mine), 0.0)
        prefix = e * arrived
        prefix_diag = e * ends[:, :1]
        prefix_level = jnp.where(bit, theirs, 0.0)
    r = rows_of((8, width))
    sent[:, :body] = packed.astype(BF16)
    for h in range(half):
        sent[h, body:] = tail_sent(diag[h], level[h])
    before_new[:, :body] = prefix
    for h in range(half):
        before_new[h, body:] = tail_rows(prefix_diag[h], prefix_level[h])
        coef[h] = jnp.where(r == 0, a[h], jnp.where(r == 1, b[h], jnp.where(r == 2, e[h], 0.0)))
    if goes_on:
        t_new[:, :body] = packed
        for h in range(half):
            t_new[h, body:] = tail_rows(diag[h], level[h])


def join_state_kernel(has_prefix, goes_on, coef, t, got, *rest):
    sent, before_new = rest[has_prefix : has_prefix + 2]
    before = rest[0]
    t_new = rest[-1]
    for h in range(t.shape[0]):
        c = coef[h]
        arrived = got[h].astype(F32)
        new = c[0:1] * t[h] + c[1:2] * arrived
        if goes_on:
            t_new[h] = new
        sent[h] = new.astype(BF16)
        add = c[2:3] * arrived
        before_new[h] = before[h] + add if has_prefix else add


def prepare_kernel(ridge, ks, kt, qo, qr, fo, fr, go, gr, q_s, m_s, e_s, base):
    pairs, _, tokens, width = ks.shape
    half = pairs // 2
    core = bit_of(0)
    beta = gates(go, gr, core, half)
    level = running_sum(gates(fo, fr, core, half))
    level_t = level.T
    scale_t = jnp.exp(level_t)
    square = (tokens, tokens)
    lower = rows_of(square) >= lanes_of(square)
    eye = (rows_of((width, width)) == lanes_of((width, width))).astype(F32)
    for side, qref in enumerate((qo, qr)):
        for h in range(half):
            p = h + side * half
            turned = kt[p, 0].astype(F32) + kt[p, 1].astype(F32)
            cross = dot(beside(split(turned * beta[p : p + 1])), twice(ks[p, 0]))
            base[p] = cross + ridge_of(ridge, core, h, half) * eye
            column = level_t[:, p : p + 1]
            m_s[p] = jnp.where(lower, jnp.exp(jnp.minimum(column - level[p : p + 1], 0.0)) * beta[p : p + 1], 0.0)
            e_s[p] = jnp.broadcast_to(scale_t[:, p : p + 1], square)
            q_s[p] = unit_rows(columns(qref, core, h, half, width).astype(F32))


def inverse_kernel(which, base, fo, fr, gf, before, got, s_s, p_s, a_s):
    half, width, _ = gf.shape
    body = width // 2
    pairs = 2 * half
    core = bit_of(0)
    first = core == 0
    bit = bit_of(which) == 1
    forget = gates(fo, fr, core, half)
    decay = jnp.exp(jnp.sum(forget, axis=1, keepdims=True))
    eye = (rows_of((width, width)) == lanes_of((width, width))).astype(F32)
    for h in range(half):
        tail = before[h, body:]
        ends = got[h, body:].astype(F32)
        e = jnp.where(bit, jnp.exp(tail[1:2]), 0.0)
        start = unpack(before[h, :body] + e * got[h, :body].astype(F32), tail[:1] + e * ends[:1])
        for side, is_early in enumerate((first, jnp.logical_not(first))):
            p = h + side * half
            other = h + (1 - side) * half
            gram = jnp.where(is_early, start, decay[other : other + 1] * start + gf[h])
            s_s[p, 0], s_s[p, 1] = split(gram)
            system = gram + base[p]
            bound = jnp.max(jnp.sum(jnp.abs(system), axis=0, keepdims=True), axis=1, keepdims=True)
            a_s[p] = system.astype(BF16)
            p_s[p] = eye / bound

    def refine(_, carry):
        left = [eye - dot(a_s[p], p_s[p].astype(BF16)) for p in range(pairs)]
        for p in range(pairs):
            now = p_s[p]
            p_s[p] = now + dot(now.astype(BF16), left[p].astype(BF16))
        return carry

    lax.fori_loop(0, NEWTON - 1, refine, 0)
    for start in range(0, pairs, half):
        group = range(start, start + half)
        left = []
        for p in group:
            high = a_s[p]
            left.append(eye - dot(beside((high, high)), jnp.concatenate(split(p_s[p]), axis=0)))
        for p, rest in zip(group, left):
            now = p_s[p]
            p_s[p] = now + dot(now.astype(BF16), rest.astype(BF16))


def correct_kernel(ridge, q_s, kt, m_s, e_s, ks, s_s, p_s, vo, vr, xs, part, x_s):
    pairs, _, width = q_s.shape
    half = pairs // 2
    core = bit_of(0)

    def both_of(p, i):
        return jnp.concatenate([s_s[p, i], kt[p, i]], axis=1)

    for p in range(pairs):
        x_s[p] = dot(q_s[p].astype(BF16), p_s[p].astype(BF16))

    def correct(_, carry):
        both = [dot(x_s[p].astype(BF16), both_of(p, 0)) for p in range(pairs)]
        applied = []
        for p in range(pairs):
            scores = m_s[p] * both[p][:, width:]
            applied.append(
                e_s[p] * both[p][:, :width]
                + dot(scores.astype(BF16), ks[p, 0])
                + ridge_of(ridge, core, p % half, half) * x_s[p]
            )
        for p in range(pairs):
            x_s[p] = x_s[p] + dot((q_s[p] - applied[p]).astype(BF16), p_s[p].astype(BF16))
        return carry

    lax.fori_loop(0, CORR - 2, correct, 0)

    for start, vref in ((0, vo), (half, vr)):
        group = range(start, start + half)
        both = [dot(wide(split(x_s[p])), tall((both_of(p, 0), both_of(p, 1)))) for p in group]
        applied = []
        for p, found in zip(group, both):
            scores = m_s[p] * found[:, width:]
            applied.append(
                e_s[p] * found[:, :width]
                + dot(scores.astype(BF16), ks[p, 0])
                + ridge_of(ridge, core, p - start, half) * x_s[p]
            )
        solved = []
        for p, found in zip(group, applied):
            x = x_s[p] + dot((q_s[p] - found).astype(BF16), p_s[p].astype(BF16))
            solved.append(split(x))
            xs[p, 0], xs[p, 1] = solved[-1]
        scores = []
        for p, x in zip(group, solved):
            scores.append(m_s[p] * dot(wide(x), tall((kt[p, 0], kt[p, 1]))))
        for p, found in zip(group, scores):
            v = columns(vref, core, p - start, half, width)
            sh, sl = split(found)
            part[p] = dot(beside((sh, sl)), twice(v))


def read_kernel(which, side, xs, part, e_s, fo, fr, uf, before_g, before, got, gain, out):
    half = uf.shape[0]
    width = uf.shape[1]
    body = width // 2
    core = bit_of(0)
    first = core == 0
    bit = bit_of(which) == 1
    decay = jnp.exp(jnp.sum(gates(fo, fr, core, half), axis=1, keepdims=True))
    is_early = jnp.logical_not(first) if side else first
    for h in range(half):
        cols = slice(h * width, (h + 1) * width)
        e = jnp.where(bit, jnp.exp(before_g[h, body + 1 : body + 2]), 0.0)
        start = before[h] + e * got[h].astype(F32)
        scale = columns(gain, core, h, half, width)
        p = h + side * half
        other = h + (1 - side) * half
        state = jnp.where(is_early, start, decay[other : other + 1] * start + uf[h])
        read = dot(wide((xs[p, 0], xs[p, 1])), tall(split(state)))
        o = e_s[p] * read + part[p]
        o = o * lax.rsqrt(jnp.mean(o * o, axis=-1, keepdims=True) + 1e-6)
        out[:, cols] = (o * scale).astype(BF16)


def stack_kernel(a, b, out):
    out[: a.shape[0]] = a[...]
    out[a.shape[0] :] = b[...]


def gathered_rows(y_own, y_other, y):
    core = bit_of(0)
    size = y_own.shape[1]
    y[:, pl.ds(pl.multiple_of(core * size, size), size)] = y_own[...]
    y[:, pl.ds(pl.multiple_of((1 - core) * size, size), size)] = y_other[...]


def project_kernel(table, chips, shares, y_own, y_other, own, other, *rest):
    result, y, out, sem = rest[-4:]
    core = bit_of(0)
    place = lax.axis_index("seq") >> 1
    share = lax.axis_index("parts")
    gathered_rows(y_own, y_other, y)
    width = 2 * own.shape[0]
    size = own.shape[1] // shares
    tokens = y.shape[0]
    lefts = []
    for offset in range(chips):
        chip = jnp.bitwise_xor(place, offset)
        rows = y[:, pl.ds(pl.multiple_of(chip * width, width), width)].astype(F32)
        rows = jnp.where(core == 0, rows, pltpu.roll(rows, width // 2, 1))
        lefts.append(rows.astype(BF16))
    copies = []
    strip = size // STRIPS
    for q in range(shares):
        for n in range(STRIPS):
            start = jnp.bitwise_xor(share, q) * size + n * strip
            where = pl.ds(pl.multiple_of(start, strip), strip)
            inner = slice(n * strip, (n + 1) * strip)
            total = jnp.zeros((tokens, strip), F32)
            for offset in range(0, chips, 2):
                blocks = []
                for o in (offset, offset + 1):
                    for flip in (0, 1):
                        if o == 0:
                            blocks.append((own, other)[flip][:, where])
                        elif (o, flip, None) in table:
                            blocks.append(rest[table[o, flip, None][0]][:, where])
                        else:
                            piece, i = table[o, flip, q]
                            blocks.append(rest[piece][i, :, inner])
                left = jnp.concatenate([lefts[offset], lefts[offset + 1]], axis=1)
                total = total + dot(left, jnp.concatenate(blocks, axis=0))
            out[:, where] = total.astype(BF16)
            copies.append(pltpu.make_async_copy(out.at[:, where], result.at[:, where], sem.at[len(copies)]))
            copies[-1].start()
    for copy in copies:
        copy.wait()


def project_copy_kernel(table, y_own, y_other, own, other, *rest):
    pieces = rest[:-4]
    out, w, y, sem = rest[-4:]
    core = bit_of(0)
    place = lax.axis_index("seq") >> 1
    share = lax.axis_index("parts")
    rows = own.shape[0]
    size = pieces[0].shape[2]

    def at(offset, flip):
        row = (jnp.bitwise_xor(place, offset) * 2 + jnp.bitwise_xor(core, flip)) * rows
        return pl.ds(pl.multiple_of(row, rows), rows)

    copies = [
        pltpu.make_async_copy(own, w.at[at(0, 0)], sem.at[0]),
        pltpu.make_async_copy(other, w.at[at(0, 1)], sem.at[1]),
    ]
    for (offset, flip, q), (piece, i) in table.items():
        where = pl.ds(pl.multiple_of(jnp.bitwise_xor(share, q) * size, size), size)
        copies.append(
            pltpu.make_async_copy(pieces[piece].at[i], w.at[at(offset, flip), where], sem.at[len(copies)])
        )
    for copy in copies:
        copy.start()
    gathered_rows(y_own, y_other, y)
    for copy in copies:
        copy.wait()
    out[...] = dot(y[...], w[...]).astype(BF16)


SMEM = pltpu.SMEM


def call(kernel, outs, scalars, ins, scratch=(), far=(), out_space=VMEM):
    spec = pl.BlockSpec(memory_space=VMEM)
    near = [pltpu.with_memory_space_constraint(a, VMEM) for a in ins]
    far = [pltpu.with_memory_space_constraint(a, pltpu.HBM) for a in far]
    return pl.pallas_call(
        kernel,
        out_shape=outs,
        in_specs=[pl.BlockSpec(memory_space=SMEM)] * len(scalars)
        + [spec] * len(near)
        + [pl.BlockSpec(memory_space=pltpu.HBM)] * len(far),
        out_specs=jax.tree.map(lambda _: pl.BlockSpec(memory_space=out_space), outs),
        scratch_shapes=scratch,
        compiler_params=pltpu.CompilerParams(vmem_limit_bytes=GRANT),
    )(*scalars, *near, *far)


def on_device(mesh, queries, keys, values, log_forget, input_gate, ridge, gain, out_weight):
    sections, parts = mesh.shape["seq"], mesh.shape["parts"]
    tokens, features = keys.shape
    heads = log_forget.shape[0]
    width = features // heads
    half = heads // 2
    pairs = 2 * half
    body = width // 2
    chips = sections // 2
    bits = chips.bit_length() - 1
    rows, out_columns = out_weight.shape

    def swap(array, distance, axis="seq"):
        count = mesh.shape[axis]
        return lax.ppermute(array, axis, [(i, i ^ distance) for i in range(count)])

    keys_o = swap(keys, 1)
    forget_o, gate_o = swap(log_forget, 1), swap(input_gate, 1)
    values_o, queries_o = swap(values, 1), swap(queries, 1)
    mine = VMEM((tokens, half * width), BF16)
    small = VMEM(log_forget.shape, F32)
    size = out_columns // parts
    far_args = (out_weight, keys, values, queries, log_forget, input_gate)
    far_args += (gain.reshape(1, features), ridge.reshape(1, heads))
    own, keys_m, values_m, queries_m, forget_m, gate_m, gain_row, ridge_row = call(
        load_kernel,
        (VMEM((1, rows, size), BF16), mine, mine, mine, small, small, VMEM((1, features), F32), VMEM((1, heads), F32)),
        (),
        (),
        (pltpu.SemaphoreType.DMA((len(far_args),)),),
        far_args,
    )
    forgets = (forget_m, forget_o)
    gate_args = (*forgets, gate_m, gate_o)

    packed = (half, body + 8, width)
    sent = (half, body + 16, width)
    full = (half, width, width)
    many = (pairs, width, width)
    two = (pairs, 2, width, width)

    pg, tg, pw, tw, gf, uf, ks, kt = call(
        sums_kernel,
        (VMEM(sent, BF16), VMEM(packed, F32), VMEM(full, BF16), VMEM(full, F32), VMEM(full, F32), VMEM(full, F32),
         VMEM(two, BF16), VMEM(two, BF16)),
        (),
        (keys_m, keys_o, values_m, values_o, *gate_args),
    )

    before = before_w = None
    tg, tw = (tg,), (tw,)
    for r in range(bits):
        got = swap(pg, 2 << r)
        got_w = swap(pw, 2 << r)
        if r == bits - 1:
            break
        extra = () if before is None else (before,)
        goes_on = r < bits - 2
        pg, before, coef, *tg = call(
            functools.partial(join_kernel, r + 1, len(extra), goes_on),
            (VMEM(sent, BF16), VMEM(packed, F32), VMEM((half, 8, width), F32), *[VMEM(packed, F32)] * goes_on),
            (),
            (*tg, got, *extra),
        )
        extra = () if before_w is None else (before_w,)
        pw, before_w, *tw = call(
            functools.partial(join_state_kernel, len(extra), goes_on),
            (VMEM(full, BF16), VMEM(full, F32), *[VMEM(full, F32)] * goes_on),
            (),
            (coef, *tw, got_w, *extra),
        )
    last = bits

    def stack(a, b):
        return call(stack_kernel, VMEM((a.shape[0] + b.shape[0], rows, size), BF16), (), (a, b))

    table, pieces = {}, []

    def keep(offsets, q, array, flip):
        for i, offset in enumerate(offsets):
            table[offset, flip, q] = (len(pieces), i)
        pieces.append(array)

    groups = []
    if bits == 3:
        far, mid = swap(own, 8), swap(own, 4)
        farther = swap(far, 4)
        near = swap(out_weight, 2)
        both = stack(far, mid)
        groups.append(((4, 2), both))
        groups.append(((6, 7), stack(farther, swap(farther, 2))))
        keep((1,), None, near, 0)
        keep((1,), None, swap(near, 1), 1)
    else:
        held = ((0,), own)
        for bit in reversed(range(bits)):
            fresh = (tuple(o ^ (1 << bit) for o in held[0]), swap(held[1], 2 << bit))
            groups.append(fresh)
            if bit:
                held = (held[0] + fresh[0], stack(held[1], fresh[1]))
    for g, (offsets, array) in enumerate(groups):
        shares = [(0, array)]
        step = 1
        while step < parts:
            shares += [(q ^ step, swap(a, step, "parts")) for q, a in shares]
            step *= 2
        if bits == 3 and g == 0:
            shares += [(q + parts, swap(a, 2)) for q, a in shares]
        for q, a in shares:
            at = offsets if q < parts else tuple(o ^ 1 for o in offsets)
            keep(at, q % parts, a, 0)
            keep(at, q % parts, swap(a, 1), 1)
    weight_o = swap(out_weight, 1)

    q_s, m_s, e_s, base = call(
        prepare_kernel,
        (VMEM(many, F32), VMEM(many, F32), VMEM(many, F32), VMEM(many, F32)),
        (),
        (ridge_row, ks, kt, queries_m, queries_o, *gate_args),
    )
    s_s, p_s = call(
        functools.partial(inverse_kernel, last),
        (VMEM(two, BF16), VMEM(many, F32)),
        (),
        (base, *forgets, gf, before, got),
        (VMEM(many, BF16),),
    )
    xs, part = call(
        correct_kernel,
        (VMEM(two, BF16), VMEM(many, F32)),
        (),
        (ridge_row, q_s, kt, m_s, e_s, ks, s_s, p_s, values_m, values_o),
        (VMEM(many, F32),),
    )

    def read(side):
        return call(
            functools.partial(read_kernel, last, side),
            VMEM((tokens, half * width), BF16),
            (),
            (xs, part, e_s, *forgets, uf, before, before_w, got_w, gain_row),
        )

    y_got = swap(read(1), 1)
    y_own = read(0)

    result = jax.ShapeDtypeStruct((tokens, out_columns), BF16)
    y_full = VMEM((tokens, features), BF16)
    if bits == 3 and 2 * rows == width:
        return call(
            functools.partial(project_kernel, table, chips, parts),
            result,
            (),
            (y_own, y_got, out_weight, weight_o, *pieces),
            (y_full, VMEM((tokens, out_columns), BF16), pltpu.SemaphoreType.DMA((parts * STRIPS,))),
            out_space=pl.ANY,
        )
    here = pl.BlockSpec(memory_space=VMEM)
    return pl.pallas_call(
        functools.partial(project_copy_kernel, table),
        out_shape=result,
        in_specs=[here, here] + [pl.BlockSpec(memory_space=pl.ANY)] * (2 + len(pieces)),
        out_specs=here,
        scratch_shapes=[
            VMEM((features, out_columns), BF16), y_full, pltpu.SemaphoreType.DMA((2 + len(table),))
        ],
    )(y_own, y_got, out_weight, weight_o, *pieces)


def solution(mesh):
    rows = P(("parts", "seq"), None)
    gate = P(None, ("parts", "seq"))

    def body(*args):
        return on_device(mesh, *args)

    return jax.shard_map(
        body,
        mesh=mesh,
        in_specs=(rows, rows, rows, gate, gate, P(), P(), P("seq", None)),
        out_specs=rows,
        check_vma=False,
    )
```
